128 devices in a mesh: fsdp: 16 (over x_hi, y, core), loop: 8 (over z, x_lo).
Axes of the slice: x: 4 (x_hi: 2, x_lo: 2; x = x_hi * 2 + x_lo), y: 4, z: 4, core: 2. Of those that a mesh axis runs over, the one named last changes fastest.
Arguments:
- iterate: bfloat16 [8, 7168, 2048], P(None, 'fsdp', 'loop'), may hold values from -0.0625 to 0.0625
- expert_order: int32 [8], replicated, may hold values from 0 to 7, each once
Outputs:
- update: bfloat16 [8, 7168, 2048], P(None, 'fsdp', 'loop')
The draws below stay inside these ranges and needn't reach their ends.
Inputs may be any that keep to these rules, and one draw needn't show every extreme that they name: `expert_order`: each value names a different expert.
All inputs are finite; a program needn't handle non-finite values.
Results may differ from the reference program's by a relative error of at most 0.006.
Values may be sent and summed in bfloat16 or wider, within the bound.
A program may use at most 128 MiB of HBM per device.

```python
import jax
import jax.numpy as jnp
from jax import lax

D = 7168
FF = 2048
EXPERTS = 8


def block_scale(own_key, dims, shards, smallest, top_value):
    factor_of, own = 1.0, jax.random.fold_in(own_key, 6)
    for position, blocks in shards:
        steps = jnp.exp(jax.random.uniform(jax.random.fold_in(own, position), (blocks,), jnp.float32, smallest / len(shards), top_value / len(shards)))
        factor_of = factor_of * jnp.repeat(steps, dims[position] // blocks).reshape([-1 if axis == position else 1 for axis in range(len(dims))])
    return factor_of


def gaussian(own_key, shape, deviation, reach, split=(), dtype=jnp.bfloat16):
    values = deviation * jax.random.normal(own_key, shape, jnp.float32)
    if split:
        values = values * block_scale(own_key, shape, split, -0.22, 0.18)
    return jnp.clip(values, -reach, reach).astype(dtype)


def setup_inputs(seed: int = 0) -> dict:
    seeds = jax.random.split(jax.random.key(seed), 3)
    return {
        "iterate": gaussian(seeds[0], (EXPERTS, D, FF), D ** -0.5, 0.0625, ((1, 16), (2, 8))),
        "expert_order": jax.random.permutation(seeds[1], EXPERTS).astype(jnp.int32),
    }


coef_linear = 3.4445
coef_cubic = -4.7750


def reference(iterate, expert_order):
    factor = 0.2 * (D ** 0.5)

    def one_slot(which):
        matrix = lax.dynamic_index_in_dim(iterate, which.astype(jnp.int32), 0, keepdims=False)
        gram = jnp.dot(matrix.T, matrix, preferred_element_type=jnp.float32)
        gram_rounded = gram.astype(jnp.bfloat16)
        product = jnp.dot(matrix, gram_rounded, preferred_element_type=jnp.float32)
        result = factor * (coef_linear * matrix.astype(jnp.float32) + coef_cubic * product)
        return result.astype(jnp.bfloat16)

    return lax.map(one_slot, expert_order)
```

```python
import jax
import jax.numpy as jnp
from jax import lax
from jax.experimental import pallas as pl
from jax.experimental.pallas import tpu as pltpu
from jax.sharding import PartitionSpec as P

MESH = pl.DeviceIdType.MESH
D = 7168
coef_linear = 3.4445
coef_cubic = -4.775
FACTOR = 0.2 * D**0.5

EXPERTS = 8
ROWS = 448
COLS = 256
FF = 2048
SLABS = 4
SLAB = 2 * COLS
DZ = (0, 1, 3, 2)
WIDTH = tuple(SLAB * (s + 1) for s in range(SLABS))
BASE = tuple(SLAB * s * (s + 1) // 2 for s in range(SLABS))
TOTAL = BASE[-1] + WIDTH[-1]
BELOW = tuple(2 * COLS * sum(SLABS - 1 - u for u in range(s)) for s in range(SLABS))
SLICE = COLS // 8
BF16 = jnp.bfloat16
F32 = jnp.float32


def kernel(x_ref, o_ref, xe, xt, gpart, rbuf, grow, gcol, pbuf, local_sem, in_send, in_recv, fwd_send, fwd_recv,
           rs_send, rs_recv, ag_send, ag_recv, sib_send, sib_recv, out_send, out_recv):
    f, l = lax.axis_index("fsdp"), lax.axis_index("loop")
    core = lax.rem(f, 2)
    y = lax.rem(f // 2, 4)
    xh = f // 8
    z = l // 2
    xl = lax.rem(l, 2)
    flip = lambda bit: 1 - bit
    xor = lambda a, b: a + b - 2 * a * b
    mine = z * 2 + xor(xl, xh)
    e_lo = xor(xl, xh)
    q_me = xh * 4 + y
    sibling = (f + 1 - 2 * core, l)

    def plane(dz, x, c):
        return ((xh * 4 + y) * 2 + c, lax.rem(z + dz, 4) * 2 + x)

    def member(k):
        qx = xor(xh, k // 4)
        qy = lax.rem(y + lax.rem(k, 4), 4)
        return qx * 4 + qy, ((qx * 4 + qy) * 2 + core, z * 2 + xor(e_lo, qx))

    my_rows = pl.ds(pl.multiple_of(core * ROWS, ROWS), ROWS)
    block = lambda s, x: pl.ds(pl.multiple_of((2 * s + x) * COLS, COLS), COLS)

    barrier = pltpu.get_barrier_semaphore()

    def greet(device):
        pl.semaphore_signal(barrier, inc=1, device_id=device, device_id_type=MESH)

    for dz in range(4):
        for dx in range(2):
            for dc in range(2):
                if dz or dx or dc:
                    greet(plane(dz, xor(xl, dx), xor(core, dc)))
    for k in range(1, 8):
        greet(member(k)[1])
    own = pltpu.make_async_copy(x_ref.at[mine], xe.at[my_rows, block(0, xl)], local_sem.at[0])
    own.start()
    pl.semaphore_wait(barrier, 22)

    def in_copy(s, dx):
        back = (4 - DZ[s]) % 4
        x = xor(xl, dx)
        expert = lax.rem(z + back, 4) * 2 + xor(x, xh)
        return pltpu.make_async_remote_copy(
            x_ref.at[expert], xe.at[my_rows, block(s, xl)], in_send.at[s, dx], in_recv.at[s, dx],
            device_id=plane(back, x, core), device_id_type=MESH)

    def in_wait(s, dx):
        there = xe.at[my_rows, block(s, xor(xl, dx))]
        pltpu.make_async_remote_copy(there, there, in_send.at[s, dx], in_recv.at[s, dx], device_id=sibling,
                                     device_id_type=MESH).wait_recv()

    def forward(s, dx):
        there = xe.at[my_rows, block(s, xor(xl, dx))]
        return pltpu.make_async_remote_copy(there, there, fwd_send.at[s, dx], fwd_recv.at[s, dx], device_id=sibling,
                                            device_id_type=MESH)

    def forward_wait(s, dx):
        other = pl.ds(pl.multiple_of((1 - core) * ROWS, ROWS), ROWS)
        there = xe.at[other, block(s, xor(xl, dx))]
        pltpu.make_async_remote_copy(there, there, fwd_send.at[s, dx], fwd_recv.at[s, dx], device_id=sibling,
                                     device_id_type=MESH).wait_recv()

    for s in range(SLABS):
        for dx in range(2):
            if s or dx:
                in_copy(s, dx).start()
    own.wait()
    forward(0, 0).start()

    def rs_copy(s, k):
        q, device = member(k)
        rows = pl.ds(pl.multiple_of(q * SLICE, SLICE), SLICE)
        cols = pl.ds(BASE[s], WIDTH[s])
        return pltpu.make_async_remote_copy(
            gpart.at[rows, cols], rbuf.at[q_me, :, cols], rs_send.at[s, q], rs_recv.at[s, q_me], device_id=device,
            device_id_type=MESH)

    def rs_wait(s, k):
        q, device = member(k)
        there = rbuf.at[q, :, pl.ds(BASE[s], WIDTH[s])]
        pltpu.make_async_remote_copy(there, there, rs_send.at[s, q], rs_recv.at[s, q], device_id=device,
                                     device_id_type=MESH).wait_recv()

    my_slice = pl.ds(pl.multiple_of(q_me * SLICE, SLICE), SLICE)

    def ag_copy(s, k):
        q, device = member(k)
        there = grow.at[my_slice, pl.ds(BASE[s], WIDTH[s])]
        return pltpu.make_async_remote_copy(there, there, ag_send.at[s, q], ag_recv.at[s, q_me], device_id=device,
                                            device_id_type=MESH)

    def ag_wait(s, k):
        q, device = member(k)
        there = grow.at[pl.ds(pl.multiple_of(q * SLICE, SLICE), SLICE), pl.ds(BASE[s], WIDTH[s])]
        pltpu.make_async_remote_copy(there, there, ag_send.at[s, q], ag_recv.at[s, q], device_id=device,
                                     device_id_type=MESH).wait_recv()

    def each_member(action):
        lax.fori_loop(1, 8, lambda k, _: (action(k), 0)[1], 0)

    for s in range(SLABS):
        for dx in range(2):
            if s or dx:
                in_wait(s, dx)
                forward(s, dx).start()
        for dx in range(2):
            forward_wait(s, dx)
        xt[...] = xe[:, block(s, core)].T

        def tiles(t, _):
            cols = pl.ds(pl.multiple_of(t * SLAB, SLAB), SLAB)
            product = jnp.dot(xt[...], xe[:, cols], preferred_element_type=F32)
            gpart[:, pl.ds(pl.multiple_of(BASE[s] + t * SLAB, SLAB), SLAB)] = product.astype(BF16)
            return 0

        lax.fori_loop(0, s + 1, tiles, 0)
        each_member(lambda k: rs_copy(s, k).start())

    for s in reversed(range(SLABS)):
        each_member(lambda k: rs_wait(s, k))

        def add(t, _):
            cols = pl.ds(pl.multiple_of(BASE[s] + t * SLAB, SLAB), SLAB)

            def term(k, total):
                return total + rbuf[member(k)[0], :, cols].astype(F32)

            total = lax.fori_loop(1, 8, term, gpart[my_slice, cols].astype(F32))
            grow[my_slice, cols] = total.astype(BF16)
            return 0

        lax.fori_loop(0, s + 1, add, 0)
        each_member(lambda k: ag_copy(s, k).start())

    def tile_at(s, t, x):
        return pl.ds(pl.multiple_of(BELOW[s] + ((t - s - 1) * 2 + x) * COLS, COLS), COLS)

    def gram_cols(s, t, x):
        return pl.ds(pl.multiple_of(BASE[t] + (2 * s + x) * COLS, COLS), COLS)

    def sib_copy(s, t):
        return pltpu.make_async_remote_copy(
            grow.at[:, gram_cols(s, t, 1 - core)], gcol.at[tile_at(s, t, core)], sib_send.at[s, t], sib_recv.at[s, t],
            device_id=sibling, device_id_type=MESH)

    def sib_wait(s, t):
        there = gcol.at[tile_at(s, t, 1 - core)]
        pltpu.make_async_remote_copy(there, there, sib_send.at[s, t], sib_recv.at[s, t], device_id=sibling,
                                     device_id_type=MESH).wait_recv()

    def out_copy(s, r):
        return pltpu.make_async_remote_copy(
            pbuf.at[s, r], o_ref.at[mine], out_send.at[s, r], out_recv.at[mine], device_id=plane(DZ[s], core, r),
            device_id_type=MESH)

    def out_wait(e):
        there = o_ref.at[e]
        pltpu.make_async_remote_copy(there, there, out_send.at[0, 0], out_recv.at[e], device_id=sibling,
                                     device_id_type=MESH).wait_recv()

    home = pltpu.make_async_copy(pbuf.at[0, core], o_ref.at[mine], local_sem.at[1])
    at_home = xl == core

    for s in reversed(range(SLABS)):
        each_member(lambda k: ag_wait(s, k))
        for u in range(s):
            sib_copy(u, s).start()
        for u in range(s):
            gcol[tile_at(u, s, core), :] = grow[:, gram_cols(u, s, core)]
        for t in range(s + 1, SLABS):
            sib_wait(s, t)

        def rows_of(r, _):
            rows = pl.ds(pl.multiple_of(r * ROWS, ROWS), ROWS)
            product = lax.dot_general(xe[rows, 0:WIDTH[s]], grow[:, BASE[s]:BASE[s] + WIDTH[s]],
                                      (((1,), (1,)), ((), ())), preferred_element_type=F32)
            if s < SLABS - 1:
                product += jnp.dot(xe[rows, WIDTH[s]:FF], gcol[BELOW[s]:BELOW[s] + FF - WIDTH[s], :],
                                   preferred_element_type=F32)
            left = xe[rows, block(s, core)].astype(F32)
            pbuf[s, r] = (FACTOR * (coef_linear * left + coef_cubic * product)).astype(BF16)
            return 0

        lax.fori_loop(0, 2, rows_of, 0)
        if s:
            for r in range(2):
                out_copy(s, r).start()
        else:
            @pl.when(at_home)
            def _():
                home.start()
                out_copy(0, 1 - core).start()

            @pl.when(jnp.logical_not(at_home))
            def _():
                for r in range(2):
                    out_copy(0, r).start()

    for s in range(SLABS):
        for dx in range(2):
            if s or dx:
                in_copy(s, dx).wait_send()
            forward(s, dx).wait_send()
        each_member(lambda k: rs_copy(s, k).wait_send())
        each_member(lambda k: ag_copy(s, k).wait_send())
        for u in range(s):
            sib_copy(u, s).wait_send()
        if s:
            for r in range(2):
                out_copy(s, r).wait_send()

    @pl.when(at_home)
    def _():
        home.wait()
        out_copy(0, 1 - core).wait_send()

    @pl.when(jnp.logical_not(at_home))
    def _():
        for r in range(2):
            out_copy(0, r).wait_send()

    for e in range(EXPERTS):
        @pl.when(jnp.logical_not(jnp.logical_and(at_home, mine == e)))
        def _():
            out_wait(e)


def exchange(iterate):
    dma = pltpu.SemaphoreType.DMA
    return pl.pallas_call(
        kernel,
        name="gram_step",
        out_shape=jax.ShapeDtypeStruct((EXPERTS, ROWS, COLS), BF16),
        in_specs=[pl.BlockSpec(memory_space=pl.ANY)],
        out_specs=pl.BlockSpec(memory_space=pl.ANY),
        scratch_shapes=[
            pltpu.VMEM((2 * ROWS, FF), BF16),
            pltpu.VMEM((COLS, 2 * ROWS), BF16),
            pltpu.VMEM((COLS, TOTAL), BF16),
            pltpu.VMEM((8, SLICE, TOTAL), BF16),
            pltpu.VMEM((COLS, TOTAL), BF16),
            pltpu.VMEM((12 * COLS, COLS), BF16),
            pltpu.VMEM((SLABS, 2, ROWS, COLS), BF16),
            dma((2,)),
            dma((SLABS, 2)), dma((SLABS, 2)),
            dma((SLABS, 2)), dma((SLABS, 2)),
            dma((SLABS, 8)), dma((SLABS, 8)),
            dma((SLABS, 8)), dma((SLABS, 8)),
            dma((SLABS, SLABS)), dma((SLABS, SLABS)),
            dma((SLABS, 2)), dma((EXPERTS,)),
        ],
        compiler_params=pltpu.CompilerParams(collective_id=0, has_side_effects=True, vmem_limit_bytes=48 << 20),
    )(iterate)


def body(iterate, expert_order):
    return jnp.take(exchange(iterate), expert_order, axis=0)


def solution(mesh):
    placed = (P(None, "fsdp", "loop"), P())
    return jax.shard_map(
        body, mesh=mesh, in_specs=placed, out_specs=P(None, "fsdp", "loop"), check_vma=False
    )
```

```python
import jax
import jax.numpy as jnp
from jax import lax
from jax.experimental import pallas as pl
from jax.experimental.pallas import tpu as pltpu
from jax.sharding import PartitionSpec as P

MESH = pl.DeviceIdType.MESH
coef_linear = 3.4445
coef_cubic = -4.775
FACTOR = 0.2 * 7168**0.5

EXPERTS = 8
ROWS = 448
COLS = 256
FF = 2048
SLABS = 4
SLAB = 2 * COLS
DZ = (0, 1, 3, 2)
WIDTH = tuple(SLAB * s + COLS + COLS * (s % 2) for s in range(SLABS))
BASE = tuple(sum(WIDTH[:s]) for s in range(SLABS))
TOTAL = sum(WIDTH)
UPTO = tuple(SLAB * s + COLS for s in range(SLABS))
BELOW = tuple(sum(FF - UPTO[u] for u in range(s)) for s in range(SLABS))
SLICE = COLS // 8
CHUNKS = ((0, 0, 256, ()), (1, 0, 1024, (0, 1)), (2, 512, 768, (1,)), (2, 0, 512, (0,)), (3, 512, 512, (1,)),
          (3, 1024, 1024, (2, 3)), (3, 0, 512, (0,)))
A, B, C, D, E, F, G = range(7)
HALF = tuple(c[2] // 2 for c in CHUNKS)
HALF_AT = tuple(sum(HALF[:n]) for n in range(len(CHUNKS)))
QUARTER = COLS // 2
BF16 = jnp.bfloat16
F32 = jnp.float32


def kernel(x_ref, o_ref, xe, xt, gpart, from_x, from_y, pair_from_y, pair_to_x, pair_kept, pair_from_x, grow, gcol, pbuf, local_sem, in_send, in_recv, fwd_send, fwd_recv,
           rs_send, rs_recv, ag_send, ag_recv, sib_send, sib_recv, out_send, out_recv):
    f, l = lax.axis_index("fsdp"), lax.axis_index("loop")
    core = lax.rem(f, 2)
    y = lax.rem(f // 2, 4)
    xh = f // 8
    z = l // 2
    xl = lax.rem(l, 2)
    xor = lambda a, b: a + b - 2 * a * b
    e_lo = xor(xl, xh)
    mine = z * 2 + e_lo
    q_me = xh * 4 + y
    sibling = (f + 1 - 2 * core, l)

    def plane(dz, x, c):
        return ((xh * 4 + y) * 2 + c, lax.rem(z + dz, 4) * 2 + x)

    def member(qx, qy):
        return ((qx * 4 + qy) * 2 + core, z * 2 + xor(e_lo, qx))

    def remote(src, dst, send, recv, device):
        return pltpu.make_async_remote_copy(src, dst, send, recv, device_id=device, device_id_type=MESH)

    def arrived(there, recv):
        remote(there, there, recv, recv, sibling).wait_recv()

    my_rows = pl.ds(pl.multiple_of(core * ROWS, ROWS), ROWS)
    other_rows = pl.ds(pl.multiple_of((1 - core) * ROWS, ROWS), ROWS)
    block = lambda s, pos: pl.ds(pl.multiple_of((2 * s + pos) * COLS, COLS), COLS)

    barrier = pltpu.get_barrier_semaphore()

    def greet(device):
        pl.semaphore_signal(barrier, inc=1, device_id=device, device_id_type=MESH)

    def other_member(k):
        qx = xor(xh, k // 4)
        qy = lax.rem(y + k % 4, 4)
        return qx * 4 + qy, member(qx, qy)

    def each_member(action):
        for k in (4, 1, 3, 5, 7, 2, 6):
            action(k)

    for dz in range(4):
        for dx in range(2):
            for dc in range(2):
                if dz or dx or dc:
                    greet(plane(dz, xor(xl, dx), xor(core, dc)))
    each_member(lambda k: greet(other_member(k)[1]))
    pos_of = lambda dx: xor(xor(xl, dx), core)
    own = pltpu.make_async_copy(x_ref.at[mine], xe.at[my_rows, block(0, pos_of(0))], local_sem.at[0])
    own.start()
    pl.semaphore_wait(barrier, 22)

    def in_copy(s, dx):
        back = (4 - DZ[s]) % 4
        x = xor(xl, dx)
        expert = lax.rem(z + back, 4) * 2 + xor(x, xh)
        return remote(x_ref.at[expert], xe.at[my_rows, block(s, pos_of(0))], in_send, in_recv.at[s, dx],
                      plane(back, x, core))

    def in_wait(s, dx):
        arrived(xe.at[my_rows, block(s, pos_of(dx))], in_recv.at[s, dx])

    def forward(s, dx):
        return remote(xe.at[my_rows, block(s, pos_of(dx))], xe.at[my_rows, block(s, 1 - pos_of(dx))],
                      fwd_send, fwd_recv.at[s], sibling)

    for s in range(SLABS):
        for dx in range(2):
            if s or dx:
                in_copy(s, dx).start()
    own.wait()
    forward(0, 0).start()

    across = member(1 - xh, y)

    def along_y(action):
        for k in (1, 3, 2):
            action(lax.rem(y + k, 4))

    def columns(n):
        return pl.ds(BASE[CHUNKS[n][0]] + CHUNKS[n][1], CHUNKS[n][2])

    def halves(n):
        first, half = columns(n).start, HALF[n]
        return pl.ds(first, half), pl.ds(first + half, half), pl.ds(HALF_AT[n], half)

    def rows_of_y(w):
        return pl.ds(pl.multiple_of(w * SLICE, SLICE), SLICE)

    def rs_start(n):
        left, right, at = halves(n)
        remote(gpart.at[1 - xh, :, left], from_x.at[:, at], rs_send, rs_recv.at[n, 0], across).start()
        along_y(lambda w: remote(gpart.at[:, rows_of_y(w), right], pair_from_y.at[y, :, :, at], rs_send,
                                 rs_recv.at[n, 1], member(xh, w)).start())

    def by_columns(n, action):
        left, right, at = halves(n)

        def some(t, _):
            here = lambda base: pl.ds(pl.multiple_of(base + t * QUARTER, QUARTER), QUARTER)
            action(here(left.start), here(right.start), here(at.start))
            return 0

        lax.fori_loop(0, HALF[n] // QUARTER, some, 0)

    def middle(n):
        left, right, at = halves(n)
        arrived(from_x.at[:, at], rs_recv.at[n, 0])

        def over_x(lc, rc, c):
            gpart[xh, :, lc] = (gpart[xh, :, lc].astype(F32) + from_x[:, c].astype(F32)).astype(BF16)

        by_columns(n, over_x)
        along_y(lambda w: remote(gpart.at[xh, rows_of_y(w), left], from_y.at[y, :, at], rs_send, rs_recv.at[n, 2],
                                 member(xh, w)).start())
        arrived(pair_from_y.at[pl.ds(0, 3), :, :, at], rs_recv.at[n, 1])

        def over_y(lc, rc, c):
            for p in range(2):
                side = xh if p else 1 - xh
                total = gpart[side, rows_of_y(y), rc].astype(F32)
                for k in (1, 3, 2):
                    total += pair_from_y[lax.rem(y + k, 4), side, :, c].astype(F32)
                if p:
                    pair_kept[:, c] = total
                else:
                    pair_to_x[:, c] = total.astype(BF16)

        by_columns(n, over_y)
        remote(pair_to_x.at[:, at], pair_from_x.at[:, at], rs_send, rs_recv.at[n, 3], across).start()

    def slab(s):
        for dx in range(2):
            if s or dx:
                in_wait(s, dx)
                forward(s, dx).start()
        arrived(xe.at[other_rows, pl.ds(2 * s * COLS, SLAB)], fwd_recv.at[s])
        xt[s % 2] = xe[:, 2 * s * COLS:(2 * s + 1) * COLS].T

    def gram(n):
        s, first, width, _ = CHUNKS[n]
        end = min(first + width, UPTO[s])
        base = BASE[s]

        def tile(t, _):
            cols = pl.ds(pl.multiple_of(t * COLS, COLS), COLS)
            product = jnp.dot(xt[s % 2], xe[:, cols], preferred_element_type=F32)
            gpart[:, :, pl.ds(pl.multiple_of(base + t * COLS, COLS), COLS)] = product.astype(BF16).reshape(2, COLS // 2, COLS)
            return 0

        lax.fori_loop(first // COLS, end // COLS, tile, 0)
        if first + width > UPTO[s]:
            product = jnp.dot(xt[core], xe[:, block(s - 1 + core, 1)], preferred_element_type=F32)
            gpart[:, :, base + UPTO[s]:base + WIDTH[s]] = product.astype(BF16).reshape(2, COLS // 2, COLS)
        rs_start(n)

    my_slice = pl.ds(pl.multiple_of(q_me * SLICE, SLICE), SLICE)

    def piece(n, qx, qy, part):
        first, width = columns(n).start, CHUNKS[n][2]
        cols = (pl.ds(first, width), pl.ds(first, width // 2), pl.ds(first + width // 2, width // 2))[part]
        return grow.at[pl.ds(pl.multiple_of((qx * 4 + qy) * SLICE, SLICE), SLICE), cols]

    def add(n):
        left, right, at = halves(n)
        arrived(from_y.at[pl.ds(0, 3), :, at], rs_recv.at[n, 2])
        arrived(pair_from_x.at[:, at], rs_recv.at[n, 3])

        def final(lc, rc, c):
            total = gpart[xh, rows_of_y(y), lc].astype(F32)
            for k in (1, 3, 2):
                total += from_y[lax.rem(y + k, 4), :, c].astype(F32)
            grow[my_slice, lc] = total.astype(BF16)
            grow[my_slice, rc] = (pair_kept[:, c] + pair_from_x[:, c].astype(F32)).astype(BF16)

        by_columns(n, final)
        mine_full = piece(n, xh, y, 0)
        remote(mine_full, mine_full, ag_send, ag_recv.at[n, 1], across).start()
        along_y(lambda w: remote(mine_full, mine_full, ag_send, ag_recv.at[n, 0], member(xh, w)).start())

    def got(n, kind, rows):
        first, width = columns(n).start, CHUNKS[n][2]
        arrived(grow.at[pl.ds(0, rows), pl.ds(first, width if kind < 2 else width // 2)], ag_recv.at[n, kind])

    def pass_on(n):
        got(n, 0, 3 * SLICE)

        def over(w):
            part = piece(n, xh, w, 1)
            remote(part, part, ag_send, ag_recv.at[n, 2], across).start()

        along_y(over)
        got(n, 1, SLICE)
        part = piece(n, 1 - xh, y, 2)
        along_y(lambda w: remote(part, part, ag_send, ag_recv.at[n, 3], member(xh, w)).start())

    def complete(n):
        got(n, 2, 3 * SLICE)
        got(n, 3, 3 * SLICE)
        t = CHUNKS[n][0]
        for u in CHUNKS[n][3]:
            if u < t or t % 2:
                sib_copy(u, t).start()
        for u in CHUNKS[n][3]:
            if u < t:
                gcol[tile_at(u, t, 0), :] = grow[:, gram_cols(u, t, 0)]
            elif t % 2:
                gcol[pair_at(t), :] = grow[:, BASE[t] + UPTO[t]:BASE[t] + WIDTH[t]].T

    def tile_at(u, t, pos):
        return pl.ds(BELOW[u] + COLS + ((t - u - 1) * 2 + pos) * COLS, COLS)

    def gram_cols(u, t, pos):
        return pl.ds(BASE[t] + (2 * u + pos) * COLS, COLS)

    def sib_copy(u, t):
        if u < t:
            return remote(grow.at[:, gram_cols(u, t, 1)], gcol.at[tile_at(u, t, 1)], sib_send, sib_recv.at[u, t], sibling)
        return remote(grow.at[:, pl.ds(BASE[t] + UPTO[t], COLS)], gcol.at[pair_at(t)], sib_send, sib_recv.at[t, t], sibling)

    def pair_at(t):
        return pl.ds(pl.multiple_of(BELOW[t - 1] + core * (BELOW[t] - BELOW[t - 1]), COLS), COLS)

    def out_copy(s, r):
        return remote(pbuf.at[2 * s + r], o_ref.at[mine], out_send, out_recv, plane(DZ[s], core, r))

    home = pltpu.make_async_copy(pbuf.at[core], o_ref.at[mine], local_sem.at[1])
    at_home = xl == core

    def product_of(s, first_of_pair=False):
        if first_of_pair:
            arrived(gcol.at[pl.ds(0, COLS)], sib_recv.at[s | 1, s | 1])
        for t in range(s + 1, SLABS):
            arrived(gcol.at[tile_at(s, t, 1)], sib_recv.at[s, t])

        def rows_of(r, _):
            rows = pl.ds(pl.multiple_of(r * ROWS, ROWS), ROWS)
            product = lax.dot_general(xe[rows, 0:UPTO[s]], grow[:, BASE[s]:BASE[s] + UPTO[s]],
                                      (((1,), (1,)), ((), ())), preferred_element_type=F32)
            product += jnp.dot(xe[rows, UPTO[s]:FF], gcol[BELOW[s]:BELOW[s] + FF - UPTO[s], :],
                               preferred_element_type=F32)
            left = xe[rows, 2 * s * COLS:(2 * s + 1) * COLS].astype(F32)
            pbuf[2 * s + r] = (FACTOR * (coef_linear * left + coef_cubic * product)).astype(BF16)
            if s:
                out_copy(s, r).start()
            else:
                stays = jnp.logical_and(at_home, r == core)

                @pl.when(stays)
                def _():
                    home.start()

                @pl.when(jnp.logical_not(stays))
                def _():
                    out_copy(s, r).start()
            return 0

        lax.fori_loop(0, 2, rows_of, 0)

    slab(0)
    gram(A)
    slab(1)
    gram(B)
    middle(A)
    slab(2)
    gram(C)
    add(A)
    gram(D)
    middle(B)
    slab(3)
    gram(F)
    gram(E)
    gram(G)
    middle(C)
    middle(D)
    middle(F)
    middle(E)
    middle(G)
    add(F)
    add(E)
    add(G)
    add(B)
    pass_on(F)
    pass_on(E)
    pass_on(G)
    add(C)
    add(D)
    complete(F)
    complete(E)
    complete(G)
    product_of(3, first_of_pair=True)
    pass_on(B)
    pass_on(C)
    pass_on(D)
    complete(B)
    complete(C)
    product_of(1, first_of_pair=True)
    complete(D)
    product_of(2, first_of_pair=False)
    pass_on(A)
    complete(A)
    product_of(0, first_of_pair=False)

    def sent(there, send):
        remote(there, there, send, send, sibling).wait_send()

    sent(x_ref.at[pl.ds(0, 7)], in_send)
    sent(xe.at[pl.ds(0, ROWS)], fwd_send)
    sent(grow.at[pl.ds(0, 7 * SLICE)], rs_send)
    sent(grow.at[pl.ds(0, 7 * SLICE)], ag_send)
    sent(gcol.at[pl.ds(0, 8 * COLS)], sib_send)

    @pl.when(at_home)
    def _():
        home.wait()
        sent(pbuf.at[pl.ds(0, 7)], out_send)
        arrived(o_ref.at[pl.ds(0, 7)], out_recv)

    @pl.when(jnp.logical_not(at_home))
    def _():
        sent(pbuf, out_send)
        arrived(o_ref, out_recv)


def exchange(iterate):
    dma = pltpu.SemaphoreType.DMA
    return pl.pallas_call(
        kernel,
        name="gram_step",
        out_shape=jax.ShapeDtypeStruct((EXPERTS, ROWS, COLS), BF16),
        in_specs=[pl.BlockSpec(memory_space=pltpu.HBM)],
        out_specs=pl.BlockSpec(memory_space=pl.ANY),
        scratch_shapes=[
            pltpu.VMEM((2 * ROWS, FF), BF16),
            pltpu.VMEM((2, COLS, 2 * ROWS), BF16),
            pltpu.VMEM((2, COLS // 2, TOTAL), BF16),
            pltpu.VMEM((COLS // 2, TOTAL // 2), BF16),
            pltpu.VMEM((4, SLICE, TOTAL // 2), BF16),
            pltpu.VMEM((4, 2, SLICE, TOTAL // 2), BF16),
            pltpu.VMEM((SLICE, TOTAL // 2), BF16),
            pltpu.VMEM((SLICE, TOTAL // 2), F32),
            pltpu.VMEM((SLICE, TOTAL // 2), BF16),
            pltpu.VMEM((COLS, TOTAL), BF16),
            pltpu.VMEM((sum(FF - u for u in UPTO), COLS), BF16),
            pltpu.VMEM((2 * SLABS, ROWS, COLS), BF16),
            dma((2,)),
            dma, dma((SLABS, 2)),
            dma, dma((SLABS,)),
            dma, dma((len(CHUNKS), 4)),
            dma, dma((len(CHUNKS), 4)),
            dma, dma((SLABS, SLABS)),
            dma, dma,
        ],
        compiler_params=pltpu.CompilerParams(collective_id=0, has_side_effects=True, vmem_limit_bytes=51 << 20),
    )(iterate)


def body(iterate, expert_order):
    return exchange(iterate).at[expert_order].get(mode="promise_in_bounds")


def solution(mesh):
    placed = (P(None, "fsdp", "loop"), P())
    return jax.shard_map(
        body, mesh=mesh, in_specs=placed, out_specs=P(None, "fsdp", "loop"), check_vma=False
    )
```

```python
import jax
import jax.numpy as jnp
from jax import lax
from jax.experimental import pallas as pl
from jax.experimental.pallas import tpu as pltpu
from jax.sharding import PartitionSpec as P

MESH = pl.DeviceIdType.MESH
coef_linear = 3.4445
coef_cubic = -4.775
FACTOR = 0.2 * 7168**0.5

EXPERTS = 8
ROWS = 448
COLS = 256
FF = 2048
SLABS = 4
SLAB = 2 * COLS
DZ = (0, 1, 3, 2)
WIDTH = tuple(SLAB * s + COLS + COLS * (s % 2) for s in range(SLABS))
BASE = tuple(sum(WIDTH[:s]) for s in range(SLABS))
TOTAL = sum(WIDTH)
UPTO = tuple(SLAB * s + COLS for s in range(SLABS))
BELOW = tuple(sum(FF - UPTO[u] for u in range(s)) for s in range(SLABS))
SLICE = COLS // 8
CHUNKS = ((0, 0, 256, ()), (1, 0, 1024, (0, 1)), (2, 512, 768, (1,)), (2, 0, 512, (0,)), (3, 512, 512, (1,)),
          (3, 1024, 1024, (2, 3)), (3, 0, 512, (0,)))
A, B, C, D, E, F, G = range(7)
HALF = tuple(c[2] // 2 for c in CHUNKS)
HALF_AT = tuple(sum(HALF[:n]) for n in range(len(CHUNKS)))
QUARTER = COLS // 2
BF16 = jnp.bfloat16
F32 = jnp.float32


def kernel(x_ref, o_ref, xe, xt, gpart, from_x, from_y, pair_from_y, pair_to_x, pair_kept, pair_from_x, grow, gcol, pbuf, local_sem, in_send, in_recv, fwd_send, fwd_recv,
           rs_send, rs_recv, ag_send, ag_recv, sib_send, sib_recv, out_send, out_recv):
    f, l = lax.axis_index("fsdp"), lax.axis_index("loop")
    core = lax.rem(f, 2)
    y = lax.rem(f // 2, 4)
    xh = f // 8
    z = l // 2
    xl = lax.rem(l, 2)
    xor = lambda a, b: a + b - 2 * a * b
    e_lo = xor(xl, xh)
    mine = z * 2 + e_lo
    q_me = xh * 4 + y
    sibling = (f + 1 - 2 * core, l)

    def plane(dz, x, c):
        return ((xh * 4 + y) * 2 + c, lax.rem(z + dz, 4) * 2 + x)

    def member(qx, qy):
        return ((qx * 4 + qy) * 2 + core, z * 2 + xor(e_lo, qx))

    def remote(src, dst, send, recv, device):
        return pltpu.make_async_remote_copy(src, dst, send, recv, device_id=device, device_id_type=MESH)

    def arrived(there, recv):
        remote(there, there, recv, recv, sibling).wait_recv()

    my_rows = pl.ds(pl.multiple_of(core * ROWS, ROWS), ROWS)
    other_rows = pl.ds(pl.multiple_of((1 - core) * ROWS, ROWS), ROWS)
    block = lambda s, pos: pl.ds(pl.multiple_of((2 * s + pos) * COLS, COLS), COLS)

    barrier = pltpu.get_barrier_semaphore()

    def greet(device):
        pl.semaphore_signal(barrier, inc=1, device_id=device, device_id_type=MESH)

    def other_member(k):
        qx = xor(xh, k // 4)
        qy = lax.rem(y + k % 4, 4)
        return qx * 4 + qy, member(qx, qy)

    def each_member(action):
        for k in (4, 1, 3, 5, 7, 2, 6):
            action(k)

    for dz in (2, 1, 3, 0):
        for dx in (1, 0):
            for dc in (1, 0):
                if dz or dx or dc:
                    greet(plane(dz, xor(xl, dx), xor(core, dc)))
    each_member(lambda k: greet(other_member(k)[1]))
    pos_of = lambda dx: xor(xor(xl, dx), core)
    own = pltpu.make_async_copy(x_ref.at[mine], xe.at[my_rows, block(0, pos_of(0))], local_sem.at[0])
    own.start()
    pl.semaphore_wait(barrier, 22)

    def in_copy(s, dx):
        back = (4 - DZ[s]) % 4
        x = xor(xl, dx)
        expert = lax.rem(z + back, 4) * 2 + xor(x, xh)
        return remote(x_ref.at[expert], xe.at[my_rows, block(s, pos_of(0))], in_send, in_recv.at[s, dx],
                      plane(back, x, core))

    def in_wait(s, dx):
        arrived(xe.at[my_rows, block(s, pos_of(dx))], in_recv.at[s, dx])

    def forward(s, dx):
        return remote(xe.at[my_rows, block(s, pos_of(dx))], xe.at[my_rows, block(s, 1 - pos_of(dx))],
                      fwd_send, fwd_recv.at[s], sibling)

    for s in range(SLABS):
        for dx in range(2):
            if s or dx:
                in_copy(s, dx).start()
    own.wait()
    forward(0, 0).start()

    across = member(1 - xh, y)

    def along_y(action):
        for k in (1, 3, 2):
            action(lax.rem(y + k, 4))

    def columns(n):
        return pl.ds(BASE[CHUNKS[n][0]] + CHUNKS[n][1], CHUNKS[n][2])

    def halves(n):
        first, half = columns(n).start, HALF[n]
        return pl.ds(first, half), pl.ds(first + half, half), pl.ds(HALF_AT[n], half)

    def rows_of_y(w):
        return pl.ds(pl.multiple_of(w * SLICE, SLICE), SLICE)

    def rs_start(n):
        left, right, at = halves(n)
        remote(gpart.at[1 - xh, :, left], from_x.at[:, at], rs_send, rs_recv.at[n, 0], across).start()
        along_y(lambda w: remote(gpart.at[:, rows_of_y(w), right], pair_from_y.at[y, :, :, at], rs_send,
                                 rs_recv.at[n, 1], member(xh, w)).start())

    def by_columns(n, action):
        left, right, at = halves(n)

        def some(t, _):
            here = lambda base: pl.ds(pl.multiple_of(base + t * QUARTER, QUARTER), QUARTER)
            action(here(left.start), here(right.start), here(at.start))
            return 0

        lax.fori_loop(0, HALF[n] // QUARTER, some, 0)

    def middle(n):
        left, right, at = halves(n)
        arrived(from_x.at[:, at], rs_recv.at[n, 0])

        def over_x(lc, rc, c):
            gpart[xh, :, lc] = (gpart[xh, :, lc].astype(F32) + from_x[:, c].astype(F32)).astype(BF16)

        by_columns(n, over_x)
        along_y(lambda w: remote(gpart.at[xh, rows_of_y(w), left], from_y.at[y, :, at], rs_send, rs_recv.at[n, 2],
                                 member(xh, w)).start())
        arrived(pair_from_y.at[pl.ds(0, 3), :, :, at], rs_recv.at[n, 1])

        def over_y(lc, rc, c):
            for p in range(2):
                side = xh if p else 1 - xh
                total = gpart[side, rows_of_y(y), rc].astype(F32)
                for k in (1, 3, 2):
                    total += pair_from_y[lax.rem(y + k, 4), side, :, c].astype(F32)
                if p:
                    pair_kept[:, c] = total
                else:
                    pair_to_x[:, c] = total.astype(BF16)

        by_columns(n, over_y)
        remote(pair_to_x.at[:, at], pair_from_x.at[:, at], rs_send, rs_recv.at[n, 3], across).start()

    def slab(s):
        for dx in range(2):
            if s or dx:
                in_wait(s, dx)
                forward(s, dx).start()
        arrived(xe.at[other_rows, pl.ds(2 * s * COLS, SLAB)], fwd_recv.at[s])
        xt[s % 2] = xe[:, 2 * s * COLS:(2 * s + 1) * COLS].T

    def gram(n):
        s, first, width, _ = CHUNKS[n]
        end = min(first + width, UPTO[s])
        base = BASE[s]

        def tile(t, _):
            cols = pl.ds(pl.multiple_of(t * COLS, COLS), COLS)
            product = jnp.dot(xt[s % 2], xe[:, cols], preferred_element_type=F32)
            gpart[:, :, pl.ds(pl.multiple_of(base + t * COLS, COLS), COLS)] = product.astype(BF16).reshape(2, COLS // 2, COLS)
            return 0

        lax.fori_loop(first // COLS, end // COLS, tile, 0)
        if first + width > UPTO[s]:
            product = jnp.dot(xt[core], xe[:, block(s - 1 + core, 1)], preferred_element_type=F32)
            gpart[:, :, base + UPTO[s]:base + WIDTH[s]] = product.astype(BF16).reshape(2, COLS // 2, COLS)
        rs_start(n)

    my_slice = pl.ds(pl.multiple_of(q_me * SLICE, SLICE), SLICE)

    def piece(n, qx, qy, part):
        first, width = columns(n).start, CHUNKS[n][2]
        cols = (pl.ds(first, width), pl.ds(first, width // 2), pl.ds(first + width // 2, width // 2))[part]
        return grow.at[pl.ds(pl.multiple_of((qx * 4 + qy) * SLICE, SLICE), SLICE), cols]

    def add(n):
        left, right, at = halves(n)
        arrived(from_y.at[pl.ds(0, 3), :, at], rs_recv.at[n, 2])
        arrived(pair_from_x.at[:, at], rs_recv.at[n, 3])

        def final(lc, rc, c):
            total = gpart[xh, rows_of_y(y), lc].astype(F32)
            for k in (1, 3, 2):
                total += from_y[lax.rem(y + k, 4), :, c].astype(F32)
            grow[my_slice, lc] = total.astype(BF16)
            grow[my_slice, rc] = (pair_kept[:, c] + pair_from_x[:, c].astype(F32)).astype(BF16)

        by_columns(n, final)
        mine_full = piece(n, xh, y, 0)
        remote(mine_full, mine_full, ag_send, ag_recv.at[n, 1], across).start()
        along_y(lambda w: remote(mine_full, mine_full, ag_send, ag_recv.at[n, 0], member(xh, w)).start())

    def got(n, kind, rows):
        first, width = columns(n).start, CHUNKS[n][2]
        arrived(grow.at[pl.ds(0, rows), pl.ds(first, width if kind < 2 else width // 2)], ag_recv.at[n, kind])

    def pass_on(n):
        got(n, 0, 3 * SLICE)

        def over(w):
            part = piece(n, xh, w, 1)
            remote(part, part, ag_send, ag_recv.at[n, 2], across).start()

        along_y(over)
        got(n, 1, SLICE)
        part = piece(n, 1 - xh, y, 2)
        along_y(lambda w: remote(part, part, ag_send, ag_recv.at[n, 3], member(xh, w)).start())

    def complete(n):
        got(n, 2, 3 * SLICE)
        got(n, 3, 3 * SLICE)
        t = CHUNKS[n][0]
        for u in CHUNKS[n][3]:
            if u < t or t % 2:
                sib_copy(u, t).start()
        if t in CHUNKS[n][3] and t % 2:
            gcol[pair_at(t), :] = grow[:, BASE[t] + UPTO[t]:BASE[t] + WIDTH[t]].T

    def place(n):
        t = CHUNKS[n][0]
        for u in CHUNKS[n][3]:
            if u < t:
                gcol[tile_at(u, t, 0), :] = grow[:, gram_cols(u, t, 0)]

    def tile_at(u, t, pos):
        return pl.ds(BELOW[u] + COLS + ((t - u - 1) * 2 + pos) * COLS, COLS)

    def gram_cols(u, t, pos):
        return pl.ds(BASE[t] + (2 * u + pos) * COLS, COLS)

    def sib_copy(u, t):
        if u < t:
            return remote(grow.at[:, gram_cols(u, t, 1)], gcol.at[tile_at(u, t, 1)], sib_send, sib_recv.at[u, t], sibling)
        return remote(grow.at[:, pl.ds(BASE[t] + UPTO[t], COLS)], gcol.at[pair_at(t)], sib_send, sib_recv.at[t, t], sibling)

    def pair_at(t):
        return pl.ds(pl.multiple_of(BELOW[t - 1] + core * (BELOW[t] - BELOW[t - 1]), COLS), COLS)

    def out_copy(s, r):
        return remote(pbuf.at[2 * s + r], o_ref.at[mine], out_send, out_recv, plane(DZ[s], core, r))

    home = pltpu.make_async_copy(pbuf.at[core], o_ref.at[mine], local_sem.at[1])
    at_home = xl == core

    def product_of(s, first_of_pair=False):
        if first_of_pair:
            arrived(gcol.at[pl.ds(0, COLS)], sib_recv.at[s | 1, s | 1])
        for t in range(s + 1, SLABS):
            arrived(gcol.at[tile_at(s, t, 1)], sib_recv.at[s, t])

        def rows_of(r, _):
            rows = pl.ds(pl.multiple_of(r * ROWS, ROWS), ROWS)
            product = lax.dot_general(xe[rows, 0:UPTO[s]], grow[:, BASE[s]:BASE[s] + UPTO[s]],
                                      (((1,), (1,)), ((), ())), preferred_element_type=F32)
            product += jnp.dot(xe[rows, UPTO[s]:FF], gcol[BELOW[s]:BELOW[s] + FF - UPTO[s], :],
                               preferred_element_type=F32)
            left = xe[rows, 2 * s * COLS:(2 * s + 1) * COLS].astype(F32)
            pbuf[2 * s + r] = (FACTOR * (coef_linear * left + coef_cubic * product)).astype(BF16)
            if s:
                out_copy(s, r).start()
            else:
                stays = jnp.logical_and(at_home, r == core)

                @pl.when(stays)
                def _():
                    home.start()

                @pl.when(jnp.logical_not(stays))
                def _():
                    out_copy(s, r).start()
            return 0

        lax.fori_loop(0, 2, rows_of, 0)

    slab(0)
    gram(A)
    slab(1)
    gram(B)
    middle(A)
    slab(2)
    gram(C)
    add(A)
    gram(D)
    middle(B)
    slab(3)
    gram(F)
    gram(E)
    gram(G)
    middle(C)
    middle(D)
    middle(F)
    middle(E)
    middle(G)
    add(F)
    add(E)
    add(G)
    add(B)
    pass_on(F)
    pass_on(E)
    pass_on(G)
    add(C)
    add(D)
    complete(F)
    complete(E)
    complete(G)
    product_of(3, first_of_pair=True)
    pass_on(B)
    pass_on(C)
    pass_on(D)
    place(E)
    place(G)
    place(F)
    complete(B)
    place(B)
    complete(C)
    place(C)
    product_of(1, first_of_pair=True)
    complete(D)
    place(D)
    product_of(2, first_of_pair=False)
    pass_on(A)
    complete(A)
    product_of(0, first_of_pair=False)

    def sent(there, send):
        remote(there, there, send, send, sibling).wait_send()

    sent(x_ref.at[pl.ds(0, 7)], in_send)
    sent(xe.at[pl.ds(0, ROWS)], fwd_send)
    sent(grow.at[pl.ds(0, 7 * SLICE)], rs_send)
    sent(grow.at[pl.ds(0, 7 * SLICE)], ag_send)
    sent(gcol.at[pl.ds(0, 8 * COLS)], sib_send)

    @pl.when(at_home)
    def _():
        home.wait()
        sent(pbuf.at[pl.ds(0, 7)], out_send)
        arrived(o_ref.at[pl.ds(0, 7)], out_recv)

    @pl.when(jnp.logical_not(at_home))
    def _():
        sent(pbuf, out_send)
        arrived(o_ref, out_recv)


def exchange(iterate):
    dma = pltpu.SemaphoreType.DMA
    return pl.pallas_call(
        kernel,
        name="gram_step",
        out_shape=jax.ShapeDtypeStruct((EXPERTS, ROWS, COLS), BF16),
        in_specs=[pl.BlockSpec(memory_space=pltpu.HBM)],
        out_specs=pl.BlockSpec(memory_space=pl.ANY),
        scratch_shapes=[
            pltpu.VMEM((2 * ROWS, FF), BF16),
            pltpu.VMEM((2, COLS, 2 * ROWS), BF16),
            pltpu.VMEM((2, COLS // 2, TOTAL), BF16),
            pltpu.VMEM((COLS // 2, TOTAL // 2), BF16),
            pltpu.VMEM((4, SLICE, TOTAL // 2), BF16),
            pltpu.VMEM((4, 2, SLICE, TOTAL // 2), BF16),
            pltpu.VMEM((SLICE, TOTAL // 2), BF16),
            pltpu.VMEM((SLICE, TOTAL // 2), F32),
            pltpu.VMEM((SLICE, TOTAL // 2), BF16),
            pltpu.VMEM((COLS, TOTAL), BF16),
            pltpu.VMEM((sum(FF - u for u in UPTO), COLS), BF16),
            pltpu.VMEM((2 * SLABS, ROWS, COLS), BF16),
            dma((2,)),
            dma, dma((SLABS, 2)),
            dma, dma((SLABS,)),
            dma, dma((len(CHUNKS), 4)),
            dma, dma((len(CHUNKS), 4)),
            dma, dma((SLABS, SLABS)),
            dma, dma,
        ],
        compiler_params=pltpu.CompilerParams(collective_id=0, has_side_effects=True, vmem_limit_bytes=51 << 20),
    )(iterate)


def body(iterate, expert_order):
    slots = lax.GatherDimensionNumbers(offset_dims=(1, 2), collapsed_slice_dims=(0,), start_index_map=(0,))
    return lax.gather(exchange(iterate), expert_order[:, None], slots, (1, ROWS, COLS), mode="promise_in_bounds")


def solution(mesh):
    placed = (P(None, "fsdp", "loop"), P())
    return jax.shard_map(
        body, mesh=mesh, in_specs=placed, out_specs=P(None, "fsdp", "loop"), check_vma=False
    )
```

```python
import jax
import jax.numpy as jnp
from jax import lax
from jax.experimental import pallas as pl
from jax.experimental.pallas import tpu as pltpu
from jax.sharding import PartitionSpec as P

MESH = pl.DeviceIdType.MESH
coef_linear = 3.4445
coef_cubic = -4.775
FACTOR = 0.2 * 7168**0.5

EXPERTS = 8
ROWS = 448
COLS = 256
FF = 2048
SLABS = 4
SLAB = 2 * COLS
DZ = (0, 1, 3, 2)
WIDTH = tuple(SLAB * s + COLS + COLS * (s % 2) for s in range(SLABS))
BASE = tuple(sum(WIDTH[:s]) for s in range(SLABS))
TOTAL = sum(WIDTH)
UPTO = tuple(SLAB * s + COLS for s in range(SLABS))
BELOW = tuple(sum(FF - UPTO[u] for u in range(s)) for s in range(SLABS))
SLICE = COLS // 8
CHUNKS = ((0, 0, 256, ()), (1, 0, 1024, (0, 1)), (2, 512, 768, (1,)), (2, 0, 512, (0,)), (3, 512, 512, (1,)),
          (3, 1024, 512, (2,)), (3, 0, 512, (0,)), (3, 1536, 512, (3,)))
A, B, C, D, E, F, G, H = range(8)
HALF = tuple(c[2] // 2 for c in CHUNKS)
HALF_AT = tuple(sum(HALF[:n]) for n in range(len(CHUNKS)))
QUARTER = COLS // 2
BF16 = jnp.bfloat16
F32 = jnp.float32


def kernel(x_ref, o_ref, xe, xt, gpart, from_x, from_y, pair_from_y, pair_to_x, pair_kept, pair_from_x, grow, gcol, pbuf, local_sem, in_send, in_recv, fwd_send, fwd_recv,
           rs_send, rs_recv, ag_send, ag_recv, sib_send, sib_recv, out_send, out_recv):
    f, l = lax.axis_index("fsdp"), lax.axis_index("loop")
    core = lax.rem(f, 2)
    y = lax.rem(f // 2, 4)
    xh = f // 8
    z = l // 2
    xl = lax.rem(l, 2)
    xor = lambda a, b: a + b - 2 * a * b
    e_lo = xor(xl, xh)
    mine = z * 2 + e_lo
    q_me = xh * 4 + y
    sibling = (f + 1 - 2 * core, l)

    def plane(dz, x, c):
        return ((xh * 4 + y) * 2 + c, lax.rem(z + dz, 4) * 2 + x)

    def member(qx, qy):
        return ((qx * 4 + qy) * 2 + core, z * 2 + xor(e_lo, qx))

    def remote(src, dst, send, recv, device):
        return pltpu.make_async_remote_copy(src, dst, send, recv, device_id=device, device_id_type=MESH)

    def arrived(there, recv):
        remote(there, there, recv, recv, sibling).wait_recv()

    my_rows = pl.ds(pl.multiple_of(core * ROWS, ROWS), ROWS)
    other_rows = pl.ds(pl.multiple_of((1 - core) * ROWS, ROWS), ROWS)
    block = lambda s, pos: pl.ds(pl.multiple_of((2 * s + pos) * COLS, COLS), COLS)

    barrier = pltpu.get_barrier_semaphore()

    def greet(device):
        pl.semaphore_signal(barrier, inc=1, device_id=device, device_id_type=MESH)

    def other_member(k):
        qx = xor(xh, k // 4)
        qy = lax.rem(y + k % 4, 4)
        return qx * 4 + qy, member(qx, qy)

    def each_member(action):
        for k in (4, 1, 3, 5, 7, 2, 6):
            action(k)

    for dz in (2, 1, 3, 0):
        for dx in (1, 0):
            for dc in (1, 0):
                if dz or dx or dc:
                    greet(plane(dz, xor(xl, dx), xor(core, dc)))
    each_member(lambda k: greet(other_member(k)[1]))
    pos_of = lambda dx: xor(xor(xl, dx), core)
    own = pltpu.make_async_copy(x_ref.at[mine], xe.at[my_rows, block(0, pos_of(0))], local_sem.at[0])
    own.start()
    pl.semaphore_wait(barrier, 22)

    def in_copy(s, dx):
        back = (4 - DZ[s]) % 4
        x = xor(xl, dx)
        expert = lax.rem(z + back, 4) * 2 + xor(x, xh)
        return remote(x_ref.at[expert], xe.at[my_rows, block(s, pos_of(0))], in_send, in_recv.at[s, dx],
                      plane(back, x, core))

    def in_wait(s, dx):
        arrived(xe.at[my_rows, block(s, pos_of(dx))], in_recv.at[s, dx])

    def forward(s, dx):
        return remote(xe.at[my_rows, block(s, pos_of(dx))], xe.at[my_rows, block(s, 1 - pos_of(dx))],
                      fwd_send, fwd_recv.at[s], sibling)

    for s in range(SLABS):
        for dx in range(2):
            if s or dx:
                in_copy(s, dx).start()
    own.wait()
    forward(0, 0).start()

    across = member(1 - xh, y)

    def along_y(action):
        for k in (1, 3, 2):
            action(lax.rem(y + k, 4))

    def columns(n):
        return pl.ds(BASE[CHUNKS[n][0]] + CHUNKS[n][1], CHUNKS[n][2])

    def halves(n):
        first, half = columns(n).start, HALF[n]
        return pl.ds(first, half), pl.ds(first + half, half), pl.ds(HALF_AT[n], half)

    def rows_of_y(w):
        return pl.ds(pl.multiple_of(w * SLICE, SLICE), SLICE)

    def rs_start(n):
        left, right, at = halves(n)
        remote(gpart.at[1 - xh, :, left], from_x.at[:, at], rs_send, rs_recv.at[n, 0], across).start()
        along_y(lambda w: remote(gpart.at[:, rows_of_y(w), right], pair_from_y.at[y, :, :, at], rs_send,
                                 rs_recv.at[n, 1], member(xh, w)).start())

    def by_columns(n, action):
        left, right, at = halves(n)

        def some(t, _):
            here = lambda base: pl.ds(pl.multiple_of(base + t * QUARTER, QUARTER), QUARTER)
            action(here(left.start), here(right.start), here(at.start))
            return 0

        lax.fori_loop(0, HALF[n] // QUARTER, some, 0)

    def middle(n):
        left, right, at = halves(n)
        arrived(from_x.at[:, at], rs_recv.at[n, 0])

        def over_x(lc, rc, c):
            gpart[xh, :, lc] = (gpart[xh, :, lc].astype(F32) + from_x[:, c].astype(F32)).astype(BF16)

        by_columns(n, over_x)
        along_y(lambda w: remote(gpart.at[xh, rows_of_y(w), left], from_y.at[y, :, at], rs_send, rs_recv.at[n, 2],
                                 member(xh, w)).start())
        arrived(pair_from_y.at[pl.ds(0, 3), :, :, at], rs_recv.at[n, 1])

        def over_y(lc, rc, c):
            for p in range(2):
                side = xh if p else 1 - xh
                total = gpart[side, rows_of_y(y), rc].astype(F32)
                for k in (1, 3, 2):
                    total += pair_from_y[lax.rem(y + k, 4), side, :, c].astype(F32)
                if p:
                    pair_kept[:, c] = total
                else:
                    pair_to_x[:, c] = total.astype(BF16)

        by_columns(n, over_y)
        remote(pair_to_x.at[:, at], pair_from_x.at[:, at], rs_send, rs_recv.at[n, 3], across).start()

    def slab(s):
        for dx in range(2):
            if s or dx:
                in_wait(s, dx)
                forward(s, dx).start()
        arrived(xe.at[other_rows, pl.ds(2 * s * COLS, SLAB)], fwd_recv.at[s])
        xt[s % 2] = xe[:, 2 * s * COLS:(2 * s + 1) * COLS].T

    def gram(n):
        s, first, width, _ = CHUNKS[n]
        end = min(first + width, UPTO[s])
        base = BASE[s]

        def tile(t, _):
            cols = pl.ds(pl.multiple_of(t * COLS, COLS), COLS)
            product = jnp.dot(xt[s % 2], xe[:, cols], preferred_element_type=F32)
            gpart[:, :, pl.ds(pl.multiple_of(base + t * COLS, COLS), COLS)] = product.astype(BF16).reshape(2, COLS // 2, COLS)
            return 0

        lax.fori_loop(first // COLS, end // COLS, tile, 0)
        if first + width > UPTO[s]:
            product = jnp.dot(xt[core], xe[:, block(s - 1 + core, 1)], preferred_element_type=F32)
            gpart[:, :, base + UPTO[s]:base + WIDTH[s]] = product.astype(BF16).reshape(2, COLS // 2, COLS)
        rs_start(n)

    my_slice = pl.ds(pl.multiple_of(q_me * SLICE, SLICE), SLICE)

    def piece(n, qx, qy, part):
        first, width = columns(n).start, CHUNKS[n][2]
        cols = (pl.ds(first, width), pl.ds(first, width // 2), pl.ds(first + width // 2, width // 2))[part]
        return grow.at[pl.ds(pl.multiple_of((qx * 4 + qy) * SLICE, SLICE), SLICE), cols]

    def add(n):
        left, right, at = halves(n)
        arrived(from_y.at[pl.ds(0, 3), :, at], rs_recv.at[n, 2])
        arrived(pair_from_x.at[:, at], rs_recv.at[n, 3])

        def final(lc, rc, c):
            total = gpart[xh, rows_of_y(y), lc].astype(F32)
            for k in (1, 3, 2):
                total += from_y[lax.rem(y + k, 4), :, c].astype(F32)
            grow[my_slice, lc] = total.astype(BF16)
            grow[my_slice, rc] = (pair_kept[:, c] + pair_from_x[:, c].astype(F32)).astype(BF16)

        by_columns(n, final)
        mine_full = piece(n, xh, y, 0)
        remote(mine_full, mine_full, ag_send, ag_recv.at[n, 1], across).start()
        along_y(lambda w: remote(mine_full, mine_full, ag_send, ag_recv.at[n, 0], member(xh, w)).start())

    def got(n, kind, rows):
        first, width = columns(n).start, CHUNKS[n][2]
        arrived(grow.at[pl.ds(0, rows), pl.ds(first, width if kind < 2 else width // 2)], ag_recv.at[n, kind])

    def pass_on(n):
        got(n, 0, 3 * SLICE)

        def over(w):
            part = piece(n, xh, w, 1)
            remote(part, part, ag_send, ag_recv.at[n, 2], across).start()

        along_y(over)
        got(n, 1, SLICE)
        part = piece(n, 1 - xh, y, 2)
        along_y(lambda w: remote(part, part, ag_send, ag_recv.at[n, 3], member(xh, w)).start())

    def complete(n):
        got(n, 2, 3 * SLICE)
        got(n, 3, 3 * SLICE)
        t = CHUNKS[n][0]
        for u in CHUNKS[n][3]:
            if u < t or t % 2:
                sib_copy(u, t).start()
        if t in CHUNKS[n][3] and t % 2:
            gcol[pair_at(t), :] = grow[:, BASE[t] + UPTO[t]:BASE[t] + WIDTH[t]].T

    def place(n):
        t = CHUNKS[n][0]
        for u in CHUNKS[n][3]:
            if u < t:
                gcol[tile_at(u, t, 0), :] = grow[:, gram_cols(u, t, 0)]

    def tile_at(u, t, pos):
        return pl.ds(BELOW[u] + COLS + ((t - u - 1) * 2 + pos) * COLS, COLS)

    def gram_cols(u, t, pos):
        return pl.ds(BASE[t] + (2 * u + pos) * COLS, COLS)

    def sib_copy(u, t):
        if u < t:
            return remote(grow.at[:, gram_cols(u, t, 1)], gcol.at[tile_at(u, t, 1)], sib_send, sib_recv.at[u, t], sibling)
        return remote(grow.at[:, pl.ds(BASE[t] + UPTO[t], COLS)], gcol.at[pair_at(t)], sib_send, sib_recv.at[t, t], sibling)

    def pair_at(t):
        return pl.ds(pl.multiple_of(BELOW[t - 1] + core * (BELOW[t] - BELOW[t - 1]), COLS), COLS)

    def out_copy(s, r):
        return remote(pbuf.at[2 * s + r], o_ref.at[mine], out_send, out_recv, plane(DZ[s], core, r))

    home = pltpu.make_async_copy(pbuf.at[core], o_ref.at[mine], local_sem.at[1])
    at_home = xl == core

    def product_of(s, first_of_pair=False):
        if first_of_pair:
            arrived(gcol.at[pl.ds(0, COLS)], sib_recv.at[s | 1, s | 1])
        for t in range(s + 1, SLABS):
            arrived(gcol.at[tile_at(s, t, 1)], sib_recv.at[s, t])

        def rows_of(r, _):
            rows = pl.ds(pl.multiple_of(r * ROWS, ROWS), ROWS)
            product = lax.dot_general(xe[rows, 0:UPTO[s]], grow[:, BASE[s]:BASE[s] + UPTO[s]],
                                      (((1,), (1,)), ((), ())), preferred_element_type=F32)
            product += jnp.dot(xe[rows, UPTO[s]:FF], gcol[BELOW[s]:BELOW[s] + FF - UPTO[s], :],
                               preferred_element_type=F32)
            left = xe[rows, 2 * s * COLS:(2 * s + 1) * COLS].astype(F32)
            pbuf[2 * s + r] = (FACTOR * (coef_linear * left + coef_cubic * product)).astype(BF16)
            if s:
                out_copy(s, r).start()
            else:
                stays = jnp.logical_and(at_home, r == core)

                @pl.when(stays)
                def _():
                    home.start()

                @pl.when(jnp.logical_not(stays))
                def _():
                    out_copy(s, r).start()
            return 0

        lax.fori_loop(0, 2, rows_of, 0)

    slab(0)
    gram(A)
    slab(1)
    gram(B)
    middle(A)
    slab(2)
    gram(C)
    add(A)
    gram(D)
    middle(B)
    slab(3)
    gram(H)
    gram(F)
    gram(E)
    gram(G)
    middle(C)
    middle(D)
    middle(H)
    middle(F)
    middle(E)
    middle(G)
    add(H)
    add(F)
    add(E)
    add(G)
    add(B)
    pass_on(H)
    pass_on(F)
    pass_on(E)
    pass_on(G)
    add(C)
    add(D)
    complete(H)
    complete(F)
    complete(E)
    complete(G)
    product_of(3, first_of_pair=True)
    pass_on(B)
    pass_on(C)
    pass_on(D)
    place(E)
    place(G)
    place(F)
    complete(B)
    place(B)
    complete(C)
    place(C)
    product_of(1, first_of_pair=True)
    complete(D)
    place(D)
    product_of(2, first_of_pair=False)
    pass_on(A)
    complete(A)
    product_of(0, first_of_pair=False)

    def sent(there, send):
        remote(there, there, send, send, sibling).wait_send()

    sent(x_ref.at[pl.ds(0, 7)], in_send)
    sent(xe.at[pl.ds(0, ROWS)], fwd_send)
    sent(grow.at[pl.ds(0, 7 * SLICE)], rs_send)
    sent(grow.at[pl.ds(0, 7 * SLICE)], ag_send)
    sent(gcol.at[pl.ds(0, 8 * COLS)], sib_send)

    @pl.when(at_home)
    def _():
        home.wait()
        sent(pbuf.at[pl.ds(0, 7)], out_send)
        arrived(o_ref.at[pl.ds(0, 7)], out_recv)

    @pl.when(jnp.logical_not(at_home))
    def _():
        sent(pbuf, out_send)
        arrived(o_ref, out_recv)


def exchange(iterate):
    dma = pltpu.SemaphoreType.DMA
    return pl.pallas_call(
        kernel,
        name="gram_step",
        out_shape=jax.ShapeDtypeStruct((EXPERTS, ROWS, COLS), BF16),
        in_specs=[pl.BlockSpec(memory_space=pltpu.HBM)],
        out_specs=pl.BlockSpec(memory_space=pl.ANY),
        scratch_shapes=[
            pltpu.VMEM((2 * ROWS, FF), BF16),
            pltpu.VMEM((2, COLS, 2 * ROWS), BF16),
            pltpu.VMEM((2, COLS // 2, TOTAL), BF16),
            pltpu.VMEM((COLS // 2, TOTAL // 2), BF16),
            pltpu.VMEM((4, SLICE, TOTAL // 2), BF16),
            pltpu.VMEM((4, 2, SLICE, TOTAL // 2), BF16),
            pltpu.VMEM((SLICE, TOTAL // 2), BF16),
            pltpu.VMEM((SLICE, TOTAL // 2), F32),
            pltpu.VMEM((SLICE, TOTAL // 2), BF16),
            pltpu.VMEM((COLS, TOTAL), BF16),
            pltpu.VMEM((sum(FF - u for u in UPTO), COLS), BF16),
            pltpu.VMEM((2 * SLABS, ROWS, COLS), BF16),
            dma((2,)),
            dma, dma((SLABS, 2)),
            dma, dma((SLABS,)),
            dma, dma((len(CHUNKS), 4)),
            dma, dma((len(CHUNKS), 4)),
            dma, dma((SLABS, SLABS)),
            dma, dma,
        ],
        compiler_params=pltpu.CompilerParams(collective_id=0, has_side_effects=True, vmem_limit_bytes=51 << 20),
    )(iterate)


def body(iterate, expert_order):
    slots = lax.GatherDimensionNumbers(offset_dims=(1, 2), collapsed_slice_dims=(0,), start_index_map=(0,))
    return lax.gather(exchange(iterate), expert_order[:, None], slots, (1, ROWS, COLS), mode="promise_in_bounds")


def solution(mesh):
    placed = (P(None, "fsdp", "loop"), P())
    return jax.shard_map(
        body, mesh=mesh, in_specs=placed, out_specs=P(None, "fsdp", "loop"), check_vma=False
    )
```

```python
import jax
import jax.numpy as jnp
from jax import lax
from jax.experimental import pallas as pl
from jax.experimental.pallas import tpu as pltpu
from jax.sharding import PartitionSpec as P

MESH = pl.DeviceIdType.MESH
coef_linear = 3.4445
coef_cubic = -4.775
FACTOR = 0.2 * 7168**0.5

EXPERTS = 8
ROWS = 448
COLS = 256
FF = 2048
SLABS = 4
SLAB = 2 * COLS
DZ = (0, 1, 3, 2)
WIDTH = tuple(SLAB * s + COLS + COLS * (s % 2) for s in range(SLABS))
BASE = tuple(sum(WIDTH[:s]) for s in range(SLABS))
TOTAL = sum(WIDTH)
UPTO = tuple(SLAB * s + COLS for s in range(SLABS))
BELOW = tuple(sum(FF - UPTO[u] for u in range(s)) for s in range(SLABS))
SLICE = COLS // 8
CHUNKS = ((0, 0, 256, ()), (1, 0, 1024, (0, 1)), (2, 512, 768, (1,)), (2, 0, 512, (0,)), (3, 512, 512, (1,)),
          (3, 1024, 512, (2,)), (3, 0, 512, (0,)), (3, 1536, 512, (3,)))
A, B, C, D, E, F, G, H = range(8)
HALF = tuple(c[2] // 2 for c in CHUNKS)
HALF_AT = tuple(sum(HALF[:n]) for n in range(len(CHUNKS)))
QUARTER = COLS // 2
BF16 = jnp.bfloat16
F32 = jnp.float32


def kernel(x_ref, o_ref, xe, xt, gpart, from_x, from_y, pair_from_y, pair_to_x, pair_kept, pair_from_x, grow, gcol, pbuf, local_sem, in_send, in_recv, fwd_send, fwd_recv,
           rs_send, rs_recv, ag_send, ag_recv, sib_send, sib_recv, out_send, out_recv):
    f, l = lax.axis_index("fsdp"), lax.axis_index("loop")
    core = lax.rem(f, 2)
    y = lax.rem(f // 2, 4)
    xh = f // 8
    z = l // 2
    xl = lax.rem(l, 2)
    xor = lambda a, b: a + b - 2 * a * b
    e_lo = xor(xl, xh)
    mine = z * 2 + e_lo
    q_me = xh * 4 + y
    sibling = (f + 1 - 2 * core, l)

    def plane(dz, x, c):
        return ((xh * 4 + y) * 2 + c, lax.rem(z + dz, 4) * 2 + x)

    def member(qx, qy):
        return ((qx * 4 + qy) * 2 + core, z * 2 + xor(e_lo, qx))

    def remote(src, dst, send, recv, device):
        return pltpu.make_async_remote_copy(src, dst, send, recv, device_id=device, device_id_type=MESH)

    def arrived(there, recv):
        remote(there, there, recv, recv, sibling).wait_recv()

    my_rows = pl.ds(pl.multiple_of(core * ROWS, ROWS), ROWS)
    other_rows = pl.ds(pl.multiple_of((1 - core) * ROWS, ROWS), ROWS)
    block = lambda s, pos: pl.ds(pl.multiple_of((2 * s + pos) * COLS, COLS), COLS)

    barrier = pltpu.get_barrier_semaphore()

    def greet(device):
        pl.semaphore_signal(barrier, inc=1, device_id=device, device_id_type=MESH)

    def other_member(k):
        qx = xor(xh, k // 4)
        qy = lax.rem(y + k % 4, 4)
        return qx * 4 + qy, member(qx, qy)

    def each_member(action):
        for k in (4, 1, 3, 5, 7, 2, 6):
            action(k)

    for dz in (2, 1, 3, 0):
        for dx in (1, 0):
            for dc in (1, 0):
                if dz or dx or dc:
                    greet(plane(dz, xor(xl, dx), xor(core, dc)))
    each_member(lambda k: greet(other_member(k)[1]))
    pos_of = lambda dx: xor(xor(xl, dx), core)
    own = pltpu.make_async_copy(x_ref.at[mine], xe.at[my_rows, block(0, pos_of(0))], local_sem.at[0])
    own.start()
    pl.semaphore_wait(barrier, 22)

    def in_copy(s, dx):
        back = (4 - DZ[s]) % 4
        x = xor(xl, dx)
        expert = lax.rem(z + back, 4) * 2 + xor(x, xh)
        return remote(x_ref.at[expert], xe.at[my_rows, block(s, pos_of(0))], in_send, in_recv.at[s, dx],
                      plane(back, x, core))

    def in_wait(s, dx):
        arrived(xe.at[my_rows, block(s, pos_of(dx))], in_recv.at[s, dx])

    def forward(s, dx):
        return remote(xe.at[my_rows, block(s, pos_of(dx))], xe.at[my_rows, block(s, 1 - pos_of(dx))],
                      fwd_send, fwd_recv.at[s], sibling)

    for s in range(SLABS):
        for dx in range(2):
            if s or dx:
                in_copy(s, dx).start()
    own.wait()
    forward(0, 0).start()

    across = member(1 - xh, y)

    def along_y(action):
        for k in (1, 3, 2):
            action(lax.rem(y + k, 4))

    def columns(n):
        return pl.ds(BASE[CHUNKS[n][0]] + CHUNKS[n][1], CHUNKS[n][2])

    def halves(n):
        first, half = columns(n).start, HALF[n]
        return pl.ds(first, half), pl.ds(first + half, half), pl.ds(HALF_AT[n], half)

    def rows_of_y(w):
        return pl.ds(pl.multiple_of(w * SLICE, SLICE), SLICE)

    def rs_start(n):
        left, right, at = halves(n)
        remote(gpart.at[1 - xh, :, left], from_x.at[:, at], rs_send, rs_recv.at[n, 0], across).start()
        along_y(lambda w: remote(gpart.at[:, rows_of_y(w), right], pair_from_y.at[y, :, :, at], rs_send,
                                 rs_recv.at[n, 1], member(xh, w)).start())

    def by_columns(n, action):
        left, right, at = halves(n)

        def some(t, _):
            here = lambda base: pl.ds(pl.multiple_of(base + t * QUARTER, QUARTER), QUARTER)
            action(here(left.start), here(right.start), here(at.start))
            return 0

        lax.fori_loop(0, HALF[n] // QUARTER, some, 0)

    def middle(n):
        left, right, at = halves(n)
        arrived(from_x.at[:, at], rs_recv.at[n, 0])

        def over_x(lc, rc, c):
            gpart[xh, :, lc] = (gpart[xh, :, lc].astype(F32) + from_x[:, c].astype(F32)).astype(BF16)

        by_columns(n, over_x)
        along_y(lambda w: remote(gpart.at[xh, rows_of_y(w), left], from_y.at[y, :, at], rs_send, rs_recv.at[n, 2],
                                 member(xh, w)).start())
        arrived(pair_from_y.at[pl.ds(0, 3), :, :, at], rs_recv.at[n, 1])

        def over_y(lc, rc, c):
            for p in range(2):
                side = xh if p else 1 - xh
                total = gpart[side, rows_of_y(y), rc].astype(F32)
                for k in (1, 3, 2):
                    total += pair_from_y[lax.rem(y + k, 4), side, :, c].astype(F32)
                if p:
                    pair_kept[:, c] = total
                else:
                    pair_to_x[:, c] = total.astype(BF16)

        by_columns(n, over_y)
        remote(pair_to_x.at[:, at], pair_from_x.at[:, at], rs_send, rs_recv.at[n, 3], across).start()

    def slab(s):
        for dx in range(2):
            if s or dx:
                in_wait(s, dx)
                forward(s, dx).start()
        arrived(xe.at[other_rows, pl.ds(2 * s * COLS, SLAB)], fwd_recv.at[s])
        xt[s % 2] = xe[:, 2 * s * COLS:(2 * s + 1) * COLS].T

    def gram(n):
        s, first, width, _ = CHUNKS[n]
        end = min(first + width, UPTO[s])
        base = BASE[s]

        def tile(t, _):
            cols = pl.ds(pl.multiple_of(t * COLS, COLS), COLS)
            product = jnp.dot(xt[s % 2], xe[:, cols], preferred_element_type=F32)
            gpart[:, :, pl.ds(pl.multiple_of(base + t * COLS, COLS), COLS)] = product.astype(BF16).reshape(2, COLS // 2, COLS)
            return 0

        lax.fori_loop(first // COLS, end // COLS, tile, 0)
        if first + width > UPTO[s]:
            product = jnp.dot(xt[core], xe[:, block(s - 1 + core, 1)], preferred_element_type=F32)
            gpart[:, :, base + UPTO[s]:base + WIDTH[s]] = product.astype(BF16).reshape(2, COLS // 2, COLS)
        rs_start(n)

    my_slice = pl.ds(pl.multiple_of(q_me * SLICE, SLICE), SLICE)

    def piece(n, qx, qy, part):
        first, width = columns(n).start, CHUNKS[n][2]
        cols = (pl.ds(first, width), pl.ds(first, width // 2), pl.ds(first + width // 2, width // 2))[part]
        return grow.at[pl.ds(pl.multiple_of((qx * 4 + qy) * SLICE, SLICE), SLICE), cols]

    def add(n):
        left, right, at = halves(n)
        arrived(from_y.at[pl.ds(0, 3), :, at], rs_recv.at[n, 2])
        arrived(pair_from_x.at[:, at], rs_recv.at[n, 3])

        def final(lc, rc, c):
            total = gpart[xh, rows_of_y(y), lc].astype(F32)
            for k in (1, 3, 2):
                total += from_y[lax.rem(y + k, 4), :, c].astype(F32)
            grow[my_slice, lc] = total.astype(BF16)
            grow[my_slice, rc] = (pair_kept[:, c] + pair_from_x[:, c].astype(F32)).astype(BF16)

        by_columns(n, final)
        mine_full = piece(n, xh, y, 0)
        remote(mine_full, mine_full, ag_send, ag_recv.at[n, 1], across).start()
        for step in (1, 3, 2):
            kind = 4 if step == 2 else 0
            remote(mine_full, mine_full, ag_send, ag_recv.at[n, kind], member(xh, lax.rem(y + step, 4))).start()

    def got(n, kind, rows):
        first, width = columns(n).start, CHUNKS[n][2]
        half = kind in (2, 3)
        arrived(grow.at[pl.ds(0, rows), pl.ds(first, width // 2 if half else width)], ag_recv.at[n, kind])

    def pass_on(n):
        def over(step):
            part = piece(n, xh, lax.rem(y + step, 4), 1)
            remote(part, part, ag_send, ag_recv.at[n, 2], across).start()

        got(n, 0, 2 * SLICE)
        over(1)
        over(3)
        got(n, 1, SLICE)
        part = piece(n, 1 - xh, y, 2)
        along_y(lambda w: remote(part, part, ag_send, ag_recv.at[n, 3], member(xh, w)).start())
        got(n, 4, SLICE)
        over(2)

    def complete(n):
        got(n, 2, 3 * SLICE)
        got(n, 3, 3 * SLICE)
        t = CHUNKS[n][0]
        for u in CHUNKS[n][3]:
            if u < t or t % 2:
                sib_copy(u, t).start()
        if t in CHUNKS[n][3] and t % 2:
            gcol[pair_at(t), :] = grow[:, BASE[t] + UPTO[t]:BASE[t] + WIDTH[t]].T

    def place(n):
        t = CHUNKS[n][0]
        for u in CHUNKS[n][3]:
            if u < t:
                gcol[tile_at(u, t, 0), :] = grow[:, gram_cols(u, t, 0)]

    def tile_at(u, t, pos):
        return pl.ds(BELOW[u] + COLS + ((t - u - 1) * 2 + pos) * COLS, COLS)

    def gram_cols(u, t, pos):
        return pl.ds(BASE[t] + (2 * u + pos) * COLS, COLS)

    def sib_copy(u, t):
        if u < t:
            return remote(grow.at[:, gram_cols(u, t, 1)], gcol.at[tile_at(u, t, 1)], sib_send, sib_recv.at[u, t], sibling)
        return remote(grow.at[:, pl.ds(BASE[t] + UPTO[t], COLS)], gcol.at[pair_at(t)], sib_send, sib_recv.at[t, t], sibling)

    def pair_at(t):
        return pl.ds(pl.multiple_of(BELOW[t - 1] + core * (BELOW[t] - BELOW[t - 1]), COLS), COLS)

    def out_copy(s, r):
        return remote(pbuf.at[2 * s + r], o_ref.at[mine], out_send, out_recv, plane(DZ[s], core, r))

    home = pltpu.make_async_copy(pbuf.at[core], o_ref.at[mine], local_sem.at[1])
    at_home = xl == core

    def product_of(s, first_of_pair=False):
        if first_of_pair:
            arrived(gcol.at[pl.ds(0, COLS)], sib_recv.at[s | 1, s | 1])
        for t in range(s + 1, SLABS):
            arrived(gcol.at[tile_at(s, t, 1)], sib_recv.at[s, t])

        def rows_of(r, _):
            rows = pl.ds(pl.multiple_of(r * ROWS, ROWS), ROWS)
            product = lax.dot_general(xe[rows, 0:UPTO[s]], grow[:, BASE[s]:BASE[s] + UPTO[s]],
                                      (((1,), (1,)), ((), ())), preferred_element_type=F32)
            product += jnp.dot(xe[rows, UPTO[s]:FF], gcol[BELOW[s]:BELOW[s] + FF - UPTO[s], :],
                               preferred_element_type=F32)
            left = xe[rows, 2 * s * COLS:(2 * s + 1) * COLS].astype(F32)
            pbuf[2 * s + r] = (FACTOR * (coef_linear * left + coef_cubic * product)).astype(BF16)
            if s:
                out_copy(s, r).start()
            else:
                stays = jnp.logical_and(at_home, r == core)

                @pl.when(stays)
                def _():
                    home.start()

                @pl.when(jnp.logical_not(stays))
                def _():
                    out_copy(s, r).start()
            return 0

        lax.fori_loop(0, 2, rows_of, 0)

    slab(0)
    gram(A)
    slab(1)
    gram(B)
    middle(A)
    slab(2)
    gram(C)
    add(A)
    gram(D)
    middle(B)
    slab(3)
    gram(H)
    gram(F)
    gram(E)
    gram(G)
    middle(C)
    middle(D)
    middle(H)
    middle(F)
    middle(E)
    middle(G)
    add(H)
    add(F)
    add(E)
    add(G)
    add(B)
    pass_on(H)
    pass_on(F)
    pass_on(E)
    pass_on(G)
    add(C)
    add(D)
    complete(H)
    complete(F)
    complete(E)
    complete(G)
    product_of(3, first_of_pair=True)
    pass_on(B)
    pass_on(C)
    pass_on(D)
    place(E)
    place(G)
    place(F)
    complete(B)
    place(B)
    complete(C)
    place(C)
    product_of(1, first_of_pair=True)
    complete(D)
    place(D)
    product_of(2, first_of_pair=False)
    pass_on(A)
    complete(A)
    product_of(0, first_of_pair=False)

    def sent(there, send):
        remote(there, there, send, send, sibling).wait_send()

    sent(x_ref.at[pl.ds(0, 7)], in_send)
    sent(xe.at[pl.ds(0, ROWS)], fwd_send)
    sent(grow.at[pl.ds(0, 7 * SLICE)], rs_send)
    sent(grow.at[pl.ds(0, 7 * SLICE)], ag_send)
    sent(gcol.at[pl.ds(0, 8 * COLS)], sib_send)

    @pl.when(at_home)
    def _():
        home.wait()
        sent(pbuf.at[pl.ds(0, 7)], out_send)
        arrived(o_ref.at[pl.ds(0, 7)], out_recv)

    @pl.when(jnp.logical_not(at_home))
    def _():
        sent(pbuf, out_send)
        arrived(o_ref, out_recv)


def exchange(iterate):
    dma = pltpu.SemaphoreType.DMA
    return pl.pallas_call(
        kernel,
        name="gram_step",
        out_shape=jax.ShapeDtypeStruct((EXPERTS, ROWS, COLS), BF16),
        in_specs=[pl.BlockSpec(memory_space=pltpu.HBM)],
        out_specs=pl.BlockSpec(memory_space=pl.ANY),
        scratch_shapes=[
            pltpu.VMEM((2 * ROWS, FF), BF16),
            pltpu.VMEM((2, COLS, 2 * ROWS), BF16),
            pltpu.VMEM((2, COLS // 2, TOTAL), BF16),
            pltpu.VMEM((COLS // 2, TOTAL // 2), BF16),
            pltpu.VMEM((4, SLICE, TOTAL // 2), BF16),
            pltpu.VMEM((4, 2, SLICE, TOTAL // 2), BF16),
            pltpu.VMEM((SLICE, TOTAL // 2), BF16),
            pltpu.VMEM((SLICE, TOTAL // 2), F32),
            pltpu.VMEM((SLICE, TOTAL // 2), BF16),
            pltpu.VMEM((COLS, TOTAL), BF16),
            pltpu.VMEM((sum(FF - u for u in UPTO), COLS), BF16),
            pltpu.VMEM((2 * SLABS, ROWS, COLS), BF16),
            dma((2,)),
            dma, dma((SLABS, 2)),
            dma, dma((SLABS,)),
            dma, dma((len(CHUNKS), 4)),
            dma, dma((len(CHUNKS), 5)),
            dma, dma((SLABS, SLABS)),
            dma, dma,
        ],
        compiler_params=pltpu.CompilerParams(collective_id=0, has_side_effects=True, vmem_limit_bytes=51 << 20),
    )(iterate)


def body(iterate, expert_order):
    slots = lax.GatherDimensionNumbers(offset_dims=(1, 2), collapsed_slice_dims=(0,), start_index_map=(0,))
    return lax.gather(exchange(iterate), expert_order[:, None], slots, (1, ROWS, COLS), mode="promise_in_bounds")


def solution(mesh):
    placed = (P(None, "fsdp", "loop"), P())
    return jax.shard_map(
        body, mesh=mesh, in_specs=placed, out_specs=P(None, "fsdp", "loop"), check_vma=False
    )
```

```python
import jax
import jax.numpy as jnp
from jax import lax
from jax.experimental import pallas as pl
from jax.experimental.pallas import tpu as pltpu
from jax.sharding import PartitionSpec as P

MESH = pl.DeviceIdType.MESH
coef_linear = 3.4445
coef_cubic = -4.775
FACTOR = 0.2 * 7168**0.5

EXPERTS = 8
ROWS = 448
COLS = 256
FF = 2048
SLABS = 4
SLAB = 2 * COLS
DZ = (0, 1, 3, 2)
WIDTH = tuple(SLAB * s + COLS + COLS * (s % 2) for s in range(SLABS))
BASE = tuple(sum(WIDTH[:s]) for s in range(SLABS))
TOTAL = sum(WIDTH)
UPTO = tuple(SLAB * s + COLS for s in range(SLABS))
BELOW = tuple(sum(FF - UPTO[u] for u in range(s)) for s in range(SLABS))
SLICE = COLS // 8
CHUNKS = ((0, 0, 256, ()), (1, 0, 512, (0,)), (2, 512, 768, (1,)), (2, 0, 512, (0,)), (3, 512, 512, (1,)),
          (3, 1024, 512, (2,)), (3, 0, 512, (0,)), (3, 1536, 512, (3,)), (1, 512, 512, (1,)))
A, B, C, D, E, F, G, H, I = range(9)
HALF = tuple(c[2] // 2 for c in CHUNKS)
HALF_AT = tuple(sum(HALF[:n]) for n in range(len(CHUNKS)))
QUARTER = COLS // 2
BF16 = jnp.bfloat16
F32 = jnp.float32


def kernel(x_ref, o_ref, xe, xt, gpart, from_x, from_y, pair_from_y, pair_to_x, pair_kept, pair_from_x, grow, gcol, pbuf, local_sem, in_send, in_recv, fwd_send, fwd_recv,
           rs_send, rs_recv, ag_send, ag_recv, sib_send, sib_recv, out_send, out_recv):
    f, l = lax.axis_index("fsdp"), lax.axis_index("loop")
    core = lax.rem(f, 2)
    y = lax.rem(f // 2, 4)
    xh = f // 8
    z = l // 2
    xl = lax.rem(l, 2)
    xor = lambda a, b: a + b - 2 * a * b
    e_lo = xor(xl, xh)
    mine = z * 2 + e_lo
    q_me = xh * 4 + y
    sibling = (f + 1 - 2 * core, l)

    def plane(dz, x, c):
        return ((xh * 4 + y) * 2 + c, lax.rem(z + dz, 4) * 2 + x)

    def member(qx, qy):
        return ((qx * 4 + qy) * 2 + core, z * 2 + xor(e_lo, qx))

    def remote(src, dst, send, recv, device):
        return pltpu.make_async_remote_copy(src, dst, send, recv, device_id=device, device_id_type=MESH)

    def arrived(there, recv):
        remote(there, there, recv, recv, sibling).wait_recv()

    my_rows = pl.ds(pl.multiple_of(core * ROWS, ROWS), ROWS)
    other_rows = pl.ds(pl.multiple_of((1 - core) * ROWS, ROWS), ROWS)
    block = lambda s, pos: pl.ds(pl.multiple_of((2 * s + pos) * COLS, COLS), COLS)

    barrier = pltpu.get_barrier_semaphore()

    def greet(device):
        pl.semaphore_signal(barrier, inc=1, device_id=device, device_id_type=MESH)

    def other_member(k):
        qx = xor(xh, k // 4)
        qy = lax.rem(y + k % 4, 4)
        return qx * 4 + qy, member(qx, qy)

    def each_member(action):
        for k in (4, 1, 3, 5, 7, 2, 6):
            action(k)

    for dz in (2, 1, 3, 0):
        for dx in (1, 0):
            for dc in (1, 0):
                if dz or dx or dc:
                    greet(plane(dz, xor(xl, dx), xor(core, dc)))
    each_member(lambda k: greet(other_member(k)[1]))
    pos_of = lambda dx: xor(xor(xl, dx), core)
    own = pltpu.make_async_copy(x_ref.at[mine], xe.at[my_rows, block(0, pos_of(0))], local_sem.at[0])
    own.start()
    pl.semaphore_wait(barrier, 22)

    def in_copy(s, dx):
        back = (4 - DZ[s]) % 4
        x = xor(xl, dx)
        expert = lax.rem(z + back, 4) * 2 + xor(x, xh)
        return remote(x_ref.at[expert], xe.at[my_rows, block(s, pos_of(0))], in_send, in_recv.at[s, dx],
                      plane(back, x, core))

    def in_wait(s, dx):
        arrived(xe.at[my_rows, block(s, pos_of(dx))], in_recv.at[s, dx])

    def forward(s, dx):
        return remote(xe.at[my_rows, block(s, pos_of(dx))], xe.at[my_rows, block(s, 1 - pos_of(dx))],
                      fwd_send, fwd_recv.at[s], sibling)

    for s in range(SLABS):
        for dx in range(2):
            if s or dx:
                in_copy(s, dx).start()
    own.wait()
    forward(0, 0).start()

    across = member(1 - xh, y)

    def along_y(action):
        for k in (1, 3, 2):
            action(lax.rem(y + k, 4))

    def columns(n):
        return pl.ds(BASE[CHUNKS[n][0]] + CHUNKS[n][1], CHUNKS[n][2])

    def halves(n):
        first, half = columns(n).start, HALF[n]
        return pl.ds(first, half), pl.ds(first + half, half), pl.ds(HALF_AT[n], half)

    def rows_of_y(w):
        return pl.ds(pl.multiple_of(w * SLICE, SLICE), SLICE)

    def rs_start(n):
        left, right, at = halves(n)
        remote(gpart.at[1 - xh, :, left], from_x.at[:, at], rs_send, rs_recv.at[n, 0], across).start()
        along_y(lambda w: remote(gpart.at[:, rows_of_y(w), right], pair_from_y.at[y, :, :, at], rs_send,
                                 rs_recv.at[n, 1], member(xh, w)).start())

    def by_columns(n, action):
        left, right, at = halves(n)

        def some(t, _):
            here = lambda base: pl.ds(pl.multiple_of(base + t * QUARTER, QUARTER), QUARTER)
            action(here(left.start), here(right.start), here(at.start))
            return 0

        lax.fori_loop(0, HALF[n] // QUARTER, some, 0)

    def middle(n):
        left, right, at = halves(n)
        arrived(from_x.at[:, at], rs_recv.at[n, 0])

        def over_x(lc, rc, c):
            gpart[xh, :, lc] = (gpart[xh, :, lc].astype(F32) + from_x[:, c].astype(F32)).astype(BF16)

        by_columns(n, over_x)
        along_y(lambda w: remote(gpart.at[xh, rows_of_y(w), left], from_y.at[y, :, at], rs_send, rs_recv.at[n, 2],
                                 member(xh, w)).start())
        arrived(pair_from_y.at[pl.ds(0, 3), :, :, at], rs_recv.at[n, 1])

        def over_y(lc, rc, c):
            for p in range(2):
                side = xh if p else 1 - xh
                total = gpart[side, rows_of_y(y), rc].astype(F32)
                for k in (1, 3, 2):
                    total += pair_from_y[lax.rem(y + k, 4), side, :, c].astype(F32)
                if p:
                    pair_kept[:, c] = total
                else:
                    pair_to_x[:, c] = total.astype(BF16)

        by_columns(n, over_y)
        remote(pair_to_x.at[:, at], pair_from_x.at[:, at], rs_send, rs_recv.at[n, 3], across).start()

    def slab(s):
        for dx in range(2):
            if s or dx:
                in_wait(s, dx)
                forward(s, dx).start()
        arrived(xe.at[other_rows, pl.ds(2 * s * COLS, SLAB)], fwd_recv.at[s])
        xt[s % 2] = xe[:, 2 * s * COLS:(2 * s + 1) * COLS].T

    def gram(n):
        s, first, width, _ = CHUNKS[n]
        end = min(first + width, UPTO[s])
        base = BASE[s]

        def tile(t, _):
            cols = pl.ds(pl.multiple_of(t * COLS, COLS), COLS)
            product = jnp.dot(xt[s % 2], xe[:, cols], preferred_element_type=F32)
            gpart[:, :, pl.ds(pl.multiple_of(base + t * COLS, COLS), COLS)] = product.astype(BF16).reshape(2, COLS // 2, COLS)
            return 0

        lax.fori_loop(first // COLS, end // COLS, tile, 0)
        if first + width > UPTO[s]:
            product = jnp.dot(xt[core], xe[:, block(s - 1 + core, 1)], preferred_element_type=F32)
            gpart[:, :, base + UPTO[s]:base + WIDTH[s]] = product.astype(BF16).reshape(2, COLS // 2, COLS)
        rs_start(n)

    my_slice = pl.ds(pl.multiple_of(q_me * SLICE, SLICE), SLICE)

    def piece(n, qx, qy, part):
        first, width = columns(n).start, CHUNKS[n][2]
        cols = (pl.ds(first, width), pl.ds(first, width // 2), pl.ds(first + width // 2, width // 2))[part]
        return grow.at[pl.ds(pl.multiple_of((qx * 4 + qy) * SLICE, SLICE), SLICE), cols]

    def add(n):
        left, right, at = halves(n)
        arrived(from_y.at[pl.ds(0, 3), :, at], rs_recv.at[n, 2])
        arrived(pair_from_x.at[:, at], rs_recv.at[n, 3])

        def final(lc, rc, c):
            total = gpart[xh, rows_of_y(y), lc].astype(F32)
            for k in (1, 3, 2):
                total += from_y[lax.rem(y + k, 4), :, c].astype(F32)
            grow[my_slice, lc] = total.astype(BF16)
            grow[my_slice, rc] = (pair_kept[:, c] + pair_from_x[:, c].astype(F32)).astype(BF16)

        by_columns(n, final)
        mine_full = piece(n, xh, y, 0)
        remote(mine_full, mine_full, ag_send, ag_recv.at[n, 1], across).start()
        along_y(lambda w: remote(mine_full, mine_full, ag_send, ag_recv.at[n, 0], member(xh, w)).start())

    def got(n, kind, rows):
        first, width = columns(n).start, CHUNKS[n][2]
        arrived(grow.at[pl.ds(0, rows), pl.ds(first, width if kind < 2 else width // 2)], ag_recv.at[n, kind])

    def pass_on(n):
        got(n, 0, 3 * SLICE)

        def over(w):
            part = piece(n, xh, w, 1)
            remote(part, part, ag_send, ag_recv.at[n, 2], across).start()

        along_y(over)
        got(n, 1, SLICE)
        part = piece(n, 1 - xh, y, 2)
        along_y(lambda w: remote(part, part, ag_send, ag_recv.at[n, 3], member(xh, w)).start())

    def complete(n):
        got(n, 2, 3 * SLICE)
        got(n, 3, 3 * SLICE)
        t = CHUNKS[n][0]
        for u in CHUNKS[n][3]:
            if u < t or t % 2:
                sib_copy(u, t).start()
        if t in CHUNKS[n][3] and t % 2:
            gcol[pair_at(t), :] = grow[:, BASE[t] + UPTO[t]:BASE[t] + WIDTH[t]].T

    def place(n):
        t = CHUNKS[n][0]
        for u in CHUNKS[n][3]:
            if u < t:
                gcol[tile_at(u, t, 0), :] = grow[:, gram_cols(u, t, 0)]

    def tile_at(u, t, pos):
        return pl.ds(BELOW[u] + COLS + ((t - u - 1) * 2 + pos) * COLS, COLS)

    def gram_cols(u, t, pos):
        return pl.ds(BASE[t] + (2 * u + pos) * COLS, COLS)

    def sib_copy(u, t):
        if u < t:
            return remote(grow.at[:, gram_cols(u, t, 1)], gcol.at[tile_at(u, t, 1)], sib_send, sib_recv.at[u, t], sibling)
        return remote(grow.at[:, pl.ds(BASE[t] + UPTO[t], COLS)], gcol.at[pair_at(t)], sib_send, sib_recv.at[t, t], sibling)

    def pair_at(t):
        return pl.ds(pl.multiple_of(BELOW[t - 1] + core * (BELOW[t] - BELOW[t - 1]), COLS), COLS)

    def out_copy(s, r):
        return remote(pbuf.at[2 * s + r], o_ref.at[mine], out_send, out_recv, plane(DZ[s], core, r))

    home = pltpu.make_async_copy(pbuf.at[core], o_ref.at[mine], local_sem.at[1])
    at_home = xl == core

    def product_of(s, first_of_pair=False):
        if first_of_pair:
            arrived(gcol.at[pl.ds(0, COLS)], sib_recv.at[s | 1, s | 1])
        for t in range(s + 1, SLABS):
            arrived(gcol.at[tile_at(s, t, 1)], sib_recv.at[s, t])

        def rows_of(r, _):
            rows = pl.ds(pl.multiple_of(r * ROWS, ROWS), ROWS)
            product = lax.dot_general(xe[rows, 0:UPTO[s]], grow[:, BASE[s]:BASE[s] + UPTO[s]],
                                      (((1,), (1,)), ((), ())), preferred_element_type=F32)
            product += jnp.dot(xe[rows, UPTO[s]:FF], gcol[BELOW[s]:BELOW[s] + FF - UPTO[s], :],
                               preferred_element_type=F32)
            left = xe[rows, 2 * s * COLS:(2 * s + 1) * COLS].astype(F32)
            pbuf[2 * s + r] = (FACTOR * (coef_linear * left + coef_cubic * product)).astype(BF16)
            if s:
                out_copy(s, r).start()
            else:
                stays = jnp.logical_and(at_home, r == core)

                @pl.when(stays)
                def _():
                    home.start()

                @pl.when(jnp.logical_not(stays))
                def _():
                    out_copy(s, r).start()
            return 0

        lax.fori_loop(0, 2, rows_of, 0)

    slab(0)
    gram(A)
    slab(1)
    gram(B)
    gram(I)
    middle(A)
    slab(2)
    gram(C)
    add(A)
    gram(D)
    middle(B)
    middle(I)
    slab(3)
    gram(H)
    gram(F)
    gram(E)
    gram(G)
    middle(C)
    middle(D)
    middle(H)
    middle(F)
    middle(E)
    middle(G)
    add(H)
    add(F)
    add(E)
    add(G)
    add(B)
    add(I)
    pass_on(H)
    pass_on(F)
    pass_on(E)
    pass_on(G)
    add(C)
    add(D)
    complete(H)
    complete(F)
    complete(E)
    complete(G)
    product_of(3, first_of_pair=True)
    pass_on(B)
    pass_on(I)
    pass_on(C)
    pass_on(D)
    place(E)
    place(G)
    place(F)
    complete(B)
    place(B)
    complete(I)
    complete(C)
    place(C)
    product_of(1, first_of_pair=True)
    complete(D)
    place(D)
    product_of(2, first_of_pair=False)
    pass_on(A)
    complete(A)
    product_of(0, first_of_pair=False)

    def sent(there, send):
        remote(there, there, send, send, sibling).wait_send()

    sent(x_ref.at[pl.ds(0, 7)], in_send)
    sent(xe.at[pl.ds(0, ROWS)], fwd_send)
    sent(grow.at[pl.ds(0, 7 * SLICE)], rs_send)
    sent(grow.at[pl.ds(0, 7 * SLICE)], ag_send)
    sent(gcol.at[pl.ds(0, 8 * COLS)], sib_send)

    @pl.when(at_home)
    def _():
        home.wait()
        sent(pbuf.at[pl.ds(0, 7)], out_send)
        arrived(o_ref.at[pl.ds(0, 7)], out_recv)

    @pl.when(jnp.logical_not(at_home))
    def _():
        sent(pbuf, out_send)
        arrived(o_ref, out_recv)


def exchange(iterate):
    dma = pltpu.SemaphoreType.DMA
    return pl.pallas_call(
        kernel,
        name="gram_step",
        out_shape=jax.ShapeDtypeStruct((EXPERTS, ROWS, COLS), BF16),
        in_specs=[pl.BlockSpec(memory_space=pltpu.HBM)],
        out_specs=pl.BlockSpec(memory_space=pl.ANY),
        scratch_shapes=[
            pltpu.VMEM((2 * ROWS, FF), BF16),
            pltpu.VMEM((2, COLS, 2 * ROWS), BF16),
            pltpu.VMEM((2, COLS // 2, TOTAL), BF16),
            pltpu.VMEM((COLS // 2, TOTAL // 2), BF16),
            pltpu.VMEM((4, SLICE, TOTAL // 2), BF16),
            pltpu.VMEM((4, 2, SLICE, TOTAL // 2), BF16),
            pltpu.VMEM((SLICE, TOTAL // 2), BF16),
            pltpu.VMEM((SLICE, TOTAL // 2), F32),
            pltpu.VMEM((SLICE, TOTAL // 2), BF16),
            pltpu.VMEM((COLS, TOTAL), BF16),
            pltpu.VMEM((sum(FF - u for u in UPTO), COLS), BF16),
            pltpu.VMEM((2 * SLABS, ROWS, COLS), BF16),
            dma((2,)),
            dma, dma((SLABS, 2)),
            dma, dma((SLABS,)),
            dma, dma((len(CHUNKS), 4)),
            dma, dma((len(CHUNKS), 4)),
            dma, dma((SLABS, SLABS)),
            dma, dma,
        ],
        compiler_params=pltpu.CompilerParams(collective_id=0, has_side_effects=True, vmem_limit_bytes=51 << 20),
    )(iterate)


def body(iterate, expert_order):
    slots = lax.GatherDimensionNumbers(offset_dims=(1, 2), collapsed_slice_dims=(0,), start_index_map=(0,))
    return lax.gather(exchange(iterate), expert_order[:, None], slots, (1, ROWS, COLS), mode="promise_in_bounds")


def solution(mesh):
    placed = (P(None, "fsdp", "loop"), P())
    return jax.shard_map(
        body, mesh=mesh, in_specs=placed, out_specs=P(None, "fsdp", "loop"), check_vma=False
    )
```
